32 devices in a mesh: tm: 4 (over y, x), space: 8 (over z, core).
Axes of the slice: x: 2, y: 2, z: 4, core: 2. Of those that a mesh axis runs over, the one named last changes fastest.
Arguments:
- init_state: float32 [512, 512], P('space'), may hold values from -6 to 6
- guess: float32 [4, 512, 512], P('tm', 'space'), may hold values from -6 to 6
- source: float32 [4, 2, 512, 512], P('tm', None, 'space'), may hold values from -6 to 6
- remap: int32 [512], P('space'), may hold values from 0 to 511, as said below
- neighbors: int32 [512, 6], P('space'), may hold values from -1 to 511, as said below
- block_class: int32 [512], P('space'), may hold values from 0 to 3
- step_number: float32 [4], replicated, may hold values from 0.3 to 3
- coarse_inverse: float32 [4, 64, 64], replicated, may hold values from -0.02 to 0.9
- coarse_step: float32 [4, 64, 64], replicated, may hold values from -0.02 to 0.99
Outputs:
- c_states: float32 [4, 512, 512], P('tm', 'space')
- f_states: float32 [4, 512, 512], P('tm', 'space')
The draws below stay inside these ranges and needn't reach their ends.
Inputs may be any that keep to these rules, and one draw needn't show every extreme that they name: `remap`: the entries are a permutation of 0 to 511. The old blocks held by one device of space (aligned runs of 64) send at most 16 blocks to the new blocks held by any one device, and every device sends exactly 16 to some device. `neighbors`: entry [b, f] is the block beside block b across face f (the planes x = 0, x = 7, y = 0, y = 7, z = 0, z = 7 of the block), or -1 at the domain's boundary or at a wall. Links are mutual. Across faces 0 to 3 the neighbour lies in the same aligned run of 64 blocks; across face 4 in the run before, across face 5 in the run after.
All inputs are finite; a program needn't handle non-finite values.
Results may differ from the reference program's by a relative error of at most 0.00018.
Values sent between devices are 32-bit elements; how exact they have to be, the bound alone decides.
A program may use at most 64 MiB of HBM per device.

```python
import math
import jax
import jax.numpy as jnp
from jax import lax

BLK = 64
CELLS = 512
FACE = 64
COARSE = 64
CLASSES = 4
FINE = 2
ITERS = 2
NB = 512
SLOTS = 16
N_TM = 4
N_SPACE = 8


def draw_remap(key, part):
    subkeys = jax.random.split(jax.random.fold_in(key, 7), 4)
    offsets = jax.random.permutation(subkeys[0], N_SPACE)
    half_size = SLOTS // 2
    imbalance = jax.random.randint(subkeys[1], (N_SPACE // 2,), -(half_size - 1), half_size)
    imbalance = imbalance.at[0].set(half_size)
    group_sizes = jnp.stack([half_size + imbalance, half_size - imbalance], axis=1).reshape(-1)
    bounds = jnp.cumsum(group_sizes)
    position = jnp.arange(BLK)
    group_of = jnp.sum((position[:, None] >= bounds[None, :]).astype(jnp.int32), axis=1)
    old_order = jax.vmap(lambda subkey: jax.random.permutation(subkey, BLK))(jax.random.split(subkeys[2], N_SPACE))
    new_order = jax.vmap(lambda subkey: jax.random.permutation(subkey, BLK))(jax.random.split(subkeys[3], N_SPACE))
    device = jnp.arange(N_SPACE)[:, None]
    target = (device + offsets[group_of][None, :]) % N_SPACE
    new_index = target * BLK + new_order[target, position[None, :]]
    old_index = device * BLK + old_order
    result = jnp.zeros((NB,), jnp.int32).at[old_index.reshape(-1)].set(new_index.reshape(-1))
    return result.astype(jnp.int32)


def draw_neighbors(key, part):
    subkeys = jax.random.split(jax.random.fold_in(key, 11), 4)
    lattice_rows = BLK // 8
    order = jax.vmap(lambda subkey: jax.random.permutation(subkey, BLK))(jax.random.split(subkeys[0], N_SPACE))
    open_x = jax.random.randint(subkeys[1], (N_SPACE, BLK), 0, 8) != 0
    open_y = jax.random.randint(subkeys[2], (N_SPACE, BLK), 0, 8) != 0
    open_z = jax.random.randint(subkeys[3], (N_SPACE, BLK), 0, 8) != 0
    site = jnp.arange(BLK)[None, :]
    layer = jnp.arange(N_SPACE)[:, None]
    site_x = site % 8
    site_y = site // 8

    def global_of(layer_at, site_at):
        layer_clip = jnp.clip(layer_at + 0 * site_at, 0, N_SPACE - 1)
        site_clip = jnp.clip(site_at + 0 * layer_at, 0, BLK - 1)
        return layer_clip * BLK + order[layer_clip, site_clip]

    def linked(valid, layer_at, site_at):
        return jnp.where(valid, global_of(layer_at, site_at), -1)
    below_layer = jnp.clip(layer - 1, 0, N_SPACE - 1)
    faces = [linked((site_x > 0) & open_x[layer, jnp.clip(site - 1, 0, BLK - 1)], layer, site - 1), linked((site_x < 7) & open_x[layer, site], layer, site + 1), linked((site_y > 0) & open_y[layer, jnp.clip(site - 8, 0, BLK - 1)], layer, site - 8), linked((site_y < lattice_rows - 1) & open_y[layer, site], layer, site + 8), linked((layer > 0) & open_z[below_layer, site], layer - 1, site), linked((layer < N_SPACE - 1) & open_z[layer, site], layer + 1, site)]
    stacked = jnp.stack(faces, axis=2)
    row_index = layer * BLK + order
    table = jnp.full((NB, 6), -1, jnp.int32).at[row_index.reshape(-1)].set(stacked.reshape(-1, 6))
    return table.astype(jnp.int32)


def coarse_matrix(key, lowest, topmost, off_spread):
    subkeys = jax.random.split(key, 2)
    diagonal = jax.random.uniform(subkeys[0], (CLASSES, COARSE), jnp.float32, lowest, topmost)
    offdiag = jax.random.uniform(subkeys[1], (CLASSES, COARSE, COARSE), jnp.float32, -off_spread, off_spread)
    identity = jnp.eye(COARSE, dtype=jnp.float32)
    return offdiag * (1.0 - identity) + identity * diagonal[:, :, None]


def draw_coarse_inverse(key, part):
    matrix = coarse_matrix(jax.random.fold_in(key, 31), 0.15, 0.6, 0.02)
    return matrix


def draw_coarse_step(key, part):
    matrix = coarse_matrix(jax.random.fold_in(key, 37), 0.55, 0.97, 0.02)
    return matrix


def set_ends(array, own_key, low, largest):
    index_at = [jax.random.randint(jax.random.fold_in(own_key, axis), (), 0, length) for axis, length in enumerate(array.shape)]
    widest = array.shape.index(max(array.shape))
    beside = index_at[:widest] + [(index_at[widest] + 1) % array.shape[widest]] + index_at[widest + 1:]
    return array.at[tuple(index_at)].set(low).at[tuple(beside)].set(largest)


def steps_of(own_key, dims, shards, least, top_value):
    gain, own = 1.0, jax.random.fold_in(own_key, 6)
    for dim, blocks in shards:
        draws = jnp.exp(jax.random.uniform(jax.random.fold_in(own, dim), (blocks,), jnp.float32, least / len(shards), top_value / len(shards)))
        gain = gain * jnp.repeat(draws, dims[dim] // blocks).reshape([-1 if axis == dim else 1 for axis in range(len(dims))])
    return gain


def noise(key, dims, spread, reach, shards=(), held_as=jnp.bfloat16):
    gain = steps_of(key, dims, shards, -0.22, 0.18) if shards else 1.0
    drawn = jax.random.normal(key, dims, jnp.float32) * spread * gain
    return jnp.minimum(jnp.maximum(drawn, -reach), reach).astype(held_as)


def setup_inputs(seed: int = 0) -> dict:
    seeds = jax.random.split(jax.random.key(seed), 10)
    init_state = noise(seeds[0], (NB, CELLS), 1.0, 6.0, ((0, 8),), jnp.float32)
    guess = noise(seeds[1], (N_TM, NB, CELLS), 1.0, 6.0, ((0, 4), (1, 8)), jnp.float32)
    source = noise(seeds[2], (N_TM, FINE, NB, CELLS), 1.0, 6.0, ((0, 4), (2, 8)), jnp.float32)
    remap = draw_remap(jax.random.fold_in(seeds[9], 71), 0)
    neighbors = draw_neighbors(jax.random.fold_in(seeds[9], 71), 0)
    block_class = set_ends(jax.random.randint(seeds[5], (NB,), 0, CLASSES), jax.random.fold_in(seeds[5], 1), 0, CLASSES - 1).astype(jnp.int32)
    step_number = jnp.clip(jnp.exp(jax.random.uniform(seeds[6], (CLASSES,), jnp.float32, math.log(0.3), math.log(3.0))), 0.3, 3.0)
    coarse_inverse = draw_coarse_inverse(jax.random.fold_in(seeds[9], 71), 0)
    coarse_step = draw_coarse_step(jax.random.fold_in(seeds[9], 71), 0)
    return dict(init_state=init_state, guess=guess, source=source, remap=remap, neighbors=neighbors, block_class=block_class, step_number=step_number, coarse_inverse=coarse_inverse, coarse_step=coarse_step)


damping = 0.8
highest = lax.Precision.HIGHEST


def block_faces(state_now):
    num_blocks = state_now.shape[0]
    cube = state_now.reshape(num_blocks, 8, 8, 8)
    planes = [cube[:, 0], cube[:, 7], cube[:, :, 0], cube[:, :, 7], cube[:, :, :, 0], cube[:, :, :, 7]]
    return [plane.reshape(num_blocks, FACE) for plane in planes]


def ghost_faces(state_now, neighbors):
    own_faces = block_faces(state_now)
    ghosts = []
    for face_no in range(6):
        neighbor_ids = neighbors[:, face_no]
        picked = jnp.take(own_faces[face_no ^ 1], jnp.clip(neighbor_ids, 0, None), axis=0)
        ghosts.append(jnp.where(neighbor_ids[:, None] >= 0, picked, 0.0))
    return ghosts


def operate(state_now, neighbors, diffusion):
    num_blocks = state_now.shape[0]
    cube = state_now.reshape(num_blocks, 8, 8, 8)
    planes = [ghost.reshape(num_blocks, 8, 8) for ghost in ghost_faces(state_now, neighbors)]
    along_x = jnp.concatenate([planes[0][:, None], cube[:, :-1]], 1) + jnp.concatenate([cube[:, 1:], planes[1][:, None]], 1)
    along_y = jnp.concatenate([planes[2][:, :, None], cube[:, :, :-1]], 2) + jnp.concatenate([cube[:, :, 1:], planes[3][:, :, None]], 2)
    along_z = jnp.concatenate([planes[4][:, :, :, None], cube[:, :, :, :-1]], 3) + jnp.concatenate([cube[:, :, :, 1:], planes[5][:, :, :, None]], 3)
    beside_all = (along_x + along_y + along_z).reshape(num_blocks, CELLS)
    return (1.0 + 6.0 * diffusion) * state_now - diffusion * beside_all


def restrict(state_now):
    num_blocks = state_now.shape[0]
    return state_now.reshape(num_blocks, 4, 2, 4, 2, 4, 2).mean(axis=(2, 4, 6)).reshape(num_blocks, COARSE)


def prolong(coarse):
    num_blocks = coarse.shape[0]
    cube = coarse.reshape(num_blocks, 4, 4, 4)
    cube = jnp.repeat(jnp.repeat(jnp.repeat(cube, 2, axis=1), 2, axis=2), 2, axis=3)
    return cube.reshape(num_blocks, CELLS)


def apply_classes(matrices, coarse, block_class):
    summed = jnp.zeros_like(coarse)
    for class_no in range(CLASSES):
        product = jnp.dot(coarse, matrices[class_no].T, precision=highest)
        summed = summed + jnp.where(block_class[:, None] == class_no, product, 0.0)
    return summed


def vcycle(driving, neighbors, diffusion, block_class, coarse_inverse):
    diagonal = 1.0 + 6.0 * diffusion
    iterate = damping * driving / diagonal
    iterate = iterate + damping * (driving - operate(iterate, neighbors, diffusion)) / diagonal
    residue = driving - operate(iterate, neighbors, diffusion)
    iterate = iterate + prolong(apply_classes(coarse_inverse, restrict(residue), block_class))
    for sweep_no in range(2):
        iterate = iterate + damping * (driving - operate(iterate, neighbors, diffusion)) / diagonal
    return iterate


def reference(init_state, guess, source, remap, neighbors, block_class, step_number, coarse_inverse, coarse_step):
    moved_start = jnp.zeros_like(init_state).at[remap].set(init_state)
    moved_guess = jnp.zeros_like(guess).at[:, remap].set(guess)
    diffusion = step_number[block_class][:, None]
    states = [moved_guess[slice_no] for slice_no in range(N_TM)]
    fine_list = []
    for sweep_no in range(ITERS):
        fine_list = []
        residuals = []
        for slice_no in range(N_TM):
            before = moved_start if slice_no == 0 else states[slice_no - 1]
            fine_state = vcycle(before + source[slice_no, 0], neighbors, diffusion, block_class, coarse_inverse)
            residual = vcycle(fine_state + source[slice_no, 1], neighbors, diffusion, block_class, coarse_inverse) - states[slice_no]
            fine_list.append(fine_state)
            residuals.append(residual)
        carried = jnp.zeros((init_state.shape[0], COARSE), jnp.float32)
        updated = []
        for slice_no in range(N_TM):
            pushed = apply_classes(coarse_step, carried, block_class)
            updated.append(states[slice_no] + (prolong(pushed) + residuals[slice_no]))
            carried = pushed + restrict(residuals[slice_no])
        states = updated
    return jnp.stack(states), jnp.stack(fine_list)
```

```python
import functools

import jax
import jax.numpy as jnp
from jax import lax
from jax.experimental import pallas as pl
from jax.experimental.pallas import tpu as pltpu
from jax.sharding import PartitionSpec as P

CELLS = 512
COARSE = 64
CLASSES = 4
ITERS = 2
DAMP = 0.8
MESH = pl.DeviceIdType.MESH
F32 = jnp.float32
BF16 = jnp.bfloat16


def split(value):
    high = value.astype(BF16)
    return high, (value - high.astype(F32)).astype(BF16)


def dot(left, right):
    return jnp.dot(left, right, preferred_element_type=F32)


def roll(value, shift):
    shift = shift % 128
    return value if shift == 0 else pltpu.roll(value, shift, 1)


def iota(shape, dim):
    return lax.broadcasted_iota(jnp.int32, shape, dim)


def kernel(
    n_tm, n_sp, bk,
    init_ref, guess_ref, source_ref, remap_ref, nb_ref, class_ref, step_ref, inv_ref, cstep_ref,
    c_ref, f_ref,
    gb, ib, gr, ir, hs, hr, st, hand, cs, cr,
    ohl, oh4, oh5, rm, pm, mi, ms, xs, vs, zs, dif,
    gs_sem, gr_sem, is_sem, ir_sem, hs_sem, hr_sem, ts_sem, tr_sem, cs_sem, cr_sem,
):
    k = lax.axis_index("tm")
    s = lax.axis_index("space")
    nb = init_ref.shape[0]
    half = nb // 2
    rows = n_sp * bk
    bits = nb.bit_length() - 1
    steps = 4

    hr[...] = jnp.zeros_like(hr)
    barrier = pltpu.get_barrier_semaphore()
    for off in range(1, n_sp):
        pl.semaphore_signal(barrier, inc=1, device_id=(k, lax.rem(s + off, n_sp)), device_id_type=MESH)
    for off in range(1, n_tm):
        pl.semaphore_signal(barrier, inc=1, device_id=(lax.rem(k + off, n_tm), s), device_id_type=MESH)

    eye = iota((nb, nb), 0) == iota((nb, nb), 1)

    def column(row):
        return jnp.sum(jnp.where(eye, row, 0.0), axis=1, keepdims=True)

    remap_row = remap_ref[...]
    target_row = lax.shift_right_logical(remap_row, bits)
    slot_row = (remap_row - lax.shift_left(target_row, bits)).astype(F32)
    target_f = target_row.astype(F32)
    same = (column(target_f) == target_f) & (iota((nb, nb), 0) < iota((nb, nb), 1))
    pos_row = jnp.sum(jnp.where(same, 1.0, 0.0), axis=0, keepdims=True)
    send_row = target_f * float(bk) + pos_row
    chosen = iota((rows, nb), 0).astype(F32) == send_row
    send_mat = jnp.where(chosen, 1.0, 0.0)
    slot_col = jnp.sum(jnp.where(chosen, slot_row + 1.0, 0.0), axis=1, keepdims=True) - 1.0
    send_mat = jnp.concatenate([send_mat, send_mat], axis=1).astype(BF16)

    def bucketed(value):
        return dot(send_mat, jnp.concatenate(split(value), axis=0)).reshape(n_sp, bk, CELLS)

    gb[:, :, :CELLS] = bucketed(guess_ref[0])
    gb[:, :, CELLS:] = jnp.broadcast_to(slot_col, (rows, 128)).reshape(n_sp, bk, 128)

    pl.semaphore_wait(barrier, n_sp - 1 + n_tm - 1)

    def move(src, dst, ssem, rsem, off):
        to = lax.rem(s + off, n_sp)
        return pltpu.make_async_remote_copy(
            src_ref=src.at[to], dst_ref=dst.at[s], send_sem=ssem.at[off], recv_sem=rsem.at[s],
            device_id=(k, to), device_id_type=MESH)

    def landed(src, dst, ssem, rsem, off):
        origin = lax.rem(s - off + n_sp, n_sp)
        pltpu.make_async_remote_copy(
            src_ref=src.at[origin], dst_ref=dst.at[origin], send_sem=ssem.at[off],
            recv_sem=rsem.at[origin], device_id=(k, origin), device_id_type=MESH).wait_recv()

    for off in range(1, n_sp):
        move(gb, gr, gs_sem, gr_sem, off).start()
    gr[s] = gb[s]

    @pl.when(k == 0)
    def _():
        ib[...] = bucketed(init_ref[...])
        for off in range(1, n_sp):
            move(ib, ir, is_sem, ir_sem, off).start()
        ir[s] = ib[s]

    class_col = column(class_ref[...].astype(F32))
    diffusion = jnp.zeros((nb, 1), F32)
    for cl in range(CLASSES):
        diffusion = diffusion + jnp.where(class_col == float(cl), step_ref[:, cl:cl + 1], 0.0)
    dif[...] = jnp.broadcast_to(diffusion, (nb, 128))

    lane_nb = iota((nb, nb), 1)
    for face in range(6):
        shift = s * nb + (0 if face < 4 else (-nb if face == 4 else nb))
        ids = nb_ref[:, face:face + 1]
        hot = jnp.where((ids - shift == lane_nb) & (ids >= 0), 1.0, 0.0)
        hot = jnp.concatenate([hot, hot], axis=1).astype(BF16)
        if face < 4:
            ohl[face * nb:(face + 1) * nb] = hot
        elif face == 4:
            oh4[...] = hot
        else:
            oh5[...] = hot

    def parent(cell):
        return (lax.shift_right_logical(cell, 7) * 16
                + (lax.shift_right_logical(cell, 4) & 3) * 4
                + lax.shift_right_logical(cell & 7, 1))

    rm[...] = jnp.where(parent(iota((CELLS, 128), 0)) == iota((CELLS, 128), 1), 0.125, 0.0).astype(BF16)
    pm[...] = jnp.where(parent(iota((128, CELLS), 1)) == (iota((128, CELLS), 0) & 63), 1.0, 0.0).astype(BF16)
    for src, dst in ((inv_ref, mi), (cstep_ref, ms)):
        high, low = split(src[...].T)
        dst[...] = jnp.concatenate([high, high, low, jnp.zeros_like(low)], axis=0)

    lane = iota((nb, 128), 1)
    zz = lane & 7
    yy = lax.shift_right_logical(lane, 3) & 7
    left = lane < 64
    zh = zz[:half]

    def classes(coarse, mat):
        high = coarse.astype(BF16).astype(F32)
        both = high + roll(coarse - high, 64)
        product = dot(jnp.concatenate([both, high], axis=1).astype(BF16), mat[...])
        low_c = jnp.where(left, 0.0, 1.0)
        picked = (jnp.where(class_col == low_c, product[:, :128], 0.0)
                  + jnp.where(class_col == low_c + 2.0, product[:, 128:], 0.0))
        return jnp.where(left, picked + roll(picked, 64), 0.0)

    def prolong(coarse):
        high = coarse.astype(BF16).astype(F32)
        return dot((high + roll(coarse - high, 64)).astype(BF16), pm[...])

    def restrict(value):
        both = dot(jnp.concatenate(split(value), axis=0), rm[...])
        return both[:nb] + both[nb:]

    def halo_up(slot):
        return pltpu.make_async_remote_copy(
            src_ref=hs.at[slot, 0], dst_ref=hr.at[slot, 0], send_sem=hs_sem.at[slot, 0],
            recv_sem=hr_sem.at[slot, 0], device_id=(k, lax.rem(s + 1, n_sp)), device_id_type=MESH)

    def halo_down(slot):
        return pltpu.make_async_remote_copy(
            src_ref=hs.at[slot, 1], dst_ref=hr.at[slot, 1], send_sem=hs_sem.at[slot, 1],
            recv_sem=hr_sem.at[slot, 1], device_id=(k, lax.rem(s + n_sp - 1, n_sp)), device_id_type=MESH)

    def tiles_of(value):
        return [value[:, 128 * j:128 * j + 128] for j in range(4)]

    def beside(value, slot):
        tiles = tiles_of(value)
        top = bottom = jnp.zeros((nb, 128), F32)
        for j in range(4):
            top = jnp.where(zz == j, roll(tiles[j], j - 7), top)
            bottom = jnp.where(zz == j, roll(tiles[j], j), bottom)
        hs[slot, 0] = jnp.where(zh < 4, top[:half], roll(top[half:], 4))
        hs[slot, 1] = jnp.where(zh < 4, bottom[:half], roll(bottom[half:], 4))

        @pl.when(s < n_sp - 1)
        def _():
            halo_up(slot).start()

        @pl.when(s > 0)
        def _():
            halo_down(slot).start()

        xface = jnp.where(left, roll(tiles[3], 64), roll(tiles[0], 64))
        yface = jnp.zeros((nb, 128), F32)
        for j in range(4):
            yface = jnp.where(yy == j, roll(tiles[j], 8 * j - 56), yface)
            yface = jnp.where(yy == 4 + j, roll(tiles[j], 32 + 8 * j), yface)
        ghosts = dot(ohl[...], jnp.concatenate(split(jnp.concatenate([xface, yface], axis=1)), axis=0))
        turned = [roll(tile, 64) for tile in tiles]
        turned = [ghosts[:nb, :128]] + turned + [ghosts[nb:2 * nb, :128]]
        g2 = ghosts[2 * nb:3 * nb, 128:]
        g3 = ghosts[3 * nb:, 128:]
        sums = []
        for j in range(4):
            total = turned[j + 1] + jnp.where(left, turned[j], turned[j + 2])
            total = total + jnp.where(yy == 0, roll(g2, -8 * j), roll(tiles[j], 8))
            total = total + jnp.where(yy == 7, roll(g3, 24 - 8 * j), roll(tiles[j], -8))
            total = total + jnp.where(zz == 0, 0.0, roll(tiles[j], 1))
            total = total + jnp.where(zz == 7, 0.0, roll(tiles[j], -1))
            sums.append(total)

        @pl.when(s > 0)
        def _():
            halo_up(slot).wait_recv()

        @pl.when(s < n_sp - 1)
        def _():
            halo_down(slot).wait_recv()

        def across(packed, hot):
            both = jnp.concatenate([packed, roll(packed, -4)], axis=0)
            return dot(hot[...], jnp.concatenate(split(both), axis=0))

        g4 = across(hr[slot, 0], oh4)
        g5 = across(hr[slot, 1], oh5)
        for j in range(4):
            sums[j] = (sums[j] + jnp.where(zz == 0, roll(g4, -j), 0.0)
                       + jnp.where(zz == 7, roll(g5, 7 - j), 0.0))
        return jnp.concatenate(sums, axis=1)

    def wide():
        diffused = jnp.concatenate([dif[...]] * 4, axis=1)
        return diffused, 1.0 + 6.0 * diffused

    def leftover(value, slot):
        diffused, diagonal = wide()
        return vs[...] - (diagonal * value - diffused * beside(value, slot))

    def sweep(slot):
        value = xs[...]
        rest = leftover(value, slot)
        xs[...] = value + DAMP * rest / wide()[1]

    def vcycle(base):
        xs[...] = DAMP * vs[...] / wide()[1]
        sweep(base)
        value = xs[...]
        rest = leftover(value, base + 1)
        xs[...] = value + prolong(classes(restrict(rest), mi))
        lax.fori_loop(0, 2, lambda i, c: (sweep(base + 2 + i), c)[1], 0)

    for off in range(1, n_sp):
        landed(gb, gr, gs_sem, gr_sem, off)
    arrived = gr[...].reshape(rows, CELLS + 128)
    slots = arrived[:, CELLS:CELLS + nb]
    take = jnp.where(slots == iota((rows, nb), 1).astype(F32), 1.0, 0.0).T.astype(BF16)

    def settled(value):
        high, low = split(value)
        return dot(take, high) + dot(take, low)

    st[0] = settled(arrived[:, :CELLS])

    def hand_copy(it):
        return pltpu.make_async_remote_copy(
            src_ref=st.at[it], dst_ref=hand.at[it], send_sem=ts_sem.at[it], recv_sem=tr_sem.at[it],
            device_id=(lax.rem(k + 1, n_tm), s), device_id_type=MESH)

    def coarse_copy(it, off):
        return pltpu.make_async_remote_copy(
            src_ref=cs.at[it], dst_ref=cr.at[it, k], send_sem=cs_sem.at[it, off],
            recv_sem=cr_sem.at[it, k], device_id=(lax.rem(k + off, n_tm), s), device_id_type=MESH)

    def coarse_landed(it, origin):
        pltpu.make_async_remote_copy(
            src_ref=cs.at[it], dst_ref=cr.at[it, origin], send_sem=cs_sem.at[it, 0],
            recv_sem=cr_sem.at[it, origin], device_id=(lax.rem(k + 1, n_tm), s),
            device_id_type=MESH).wait_recv()

    def iteration(it, carry):
        @pl.when(k < n_tm - 1)
        def _():
            hand_copy(it).start()

        @pl.when((k == 0) & (it == 0))
        def _():
            for off in range(1, n_sp):
                landed(ib, ir, is_sem, ir_sem, off)
            start = settled(ir[...].reshape(rows, CELLS))
            for i in range(ITERS):
                hand[i] = start

        @pl.when(k > 0)
        def _():
            hand_copy(it).wait_recv()

        vs[...] = hand[it] + source_ref[0, 0]

        def one(v, c):
            vcycle((it * 2 + v) * steps)

            @pl.when(v == 0)
            def _():
                f_ref[0] = xs[...]
                vs[...] = xs[...] + source_ref[0, 1]
            return c

        lax.fori_loop(0, 2, one, 0)
        residual = xs[...] - st[it]
        cs[it] = restrict(residual)
        for off in range(1, n_tm):
            @pl.when(k + off < n_tm)
            def _():
                coarse_copy(it, off).start()
        zs[...] = jnp.zeros_like(zs)
        for j in range(n_tm - 1):
            @pl.when(j < k)
            def _():
                coarse_landed(it, j)
                zs[...] = classes(zs[...], ms) + cr[it, j]
        st[it + 1] = st[it] + (prolong(classes(zs[...], ms)) + residual)
        return carry

    lax.fori_loop(0, ITERS, iteration, 0)
    c_ref[0] = st[ITERS]

    for off in range(1, n_sp):
        move(gb, gr, gs_sem, gr_sem, off).wait_send()

    @pl.when(k == 0)
    def _():
        for off in range(1, n_sp):
            move(ib, ir, is_sem, ir_sem, off).wait_send()

    def drain(slot, carry):
        @pl.when(s < n_sp - 1)
        def _():
            halo_up(slot).wait_send()

        @pl.when(s > 0)
        def _():
            halo_down(slot).wait_send()
        return carry

    lax.fori_loop(0, ITERS * 2 * steps, drain, 0)
    for it in range(ITERS):
        @pl.when(k < n_tm - 1)
        def _():
            hand_copy(it).wait_send()
        for off in range(1, n_tm):
            @pl.when(k + off < n_tm)
            def _():
                coarse_copy(it, off).wait_send()


def solution(mesh):
    n_tm, n_sp = mesh.shape["tm"], mesh.shape["space"]

    def body(init_state, guess, source, remap, neighbors, block_class, step_number, inverse, cstep):
        nb = init_state.shape[0]
        bk = -(-(2 * nb // n_sp) // 8) * 8
        slots = ITERS * 2 * 4
        dma = pltpu.SemaphoreType.DMA
        out = jax.ShapeDtypeStruct((1, nb, CELLS), F32)
        return pl.pallas_call(
            functools.partial(kernel, n_tm, n_sp, bk),
            name="mgrit",
            out_shape=(out, out),
            in_specs=[pl.BlockSpec(memory_space=pltpu.VMEM)] * 9,
            out_specs=[pl.BlockSpec(memory_space=pltpu.VMEM)] * 2,
            scratch_shapes=[
                pltpu.VMEM((n_sp, bk, CELLS + 128), F32),
                pltpu.VMEM((n_sp, bk, CELLS), F32),
                pltpu.VMEM((n_sp, bk, CELLS + 128), F32),
                pltpu.VMEM((n_sp, bk, CELLS), F32),
                pltpu.VMEM((slots, 2, nb // 2, 128), F32),
                pltpu.VMEM((slots, 2, nb // 2, 128), F32),
                pltpu.VMEM((ITERS + 1, nb, CELLS), F32),
                pltpu.VMEM((ITERS, nb, CELLS), F32),
                pltpu.VMEM((ITERS, nb, 128), F32),
                pltpu.VMEM((ITERS, n_tm, nb, 128), F32),
                pltpu.VMEM((4 * nb, 2 * nb), BF16),
                pltpu.VMEM((nb, 2 * nb), BF16),
                pltpu.VMEM((nb, 2 * nb), BF16),
                pltpu.VMEM((CELLS, 128), BF16),
                pltpu.VMEM((128, CELLS), BF16),
                pltpu.VMEM((4 * COARSE, CLASSES * COARSE), BF16),
                pltpu.VMEM((4 * COARSE, CLASSES * COARSE), BF16),
                pltpu.VMEM((nb, CELLS), F32),
                pltpu.VMEM((nb, CELLS), F32),
                pltpu.VMEM((nb, 128), F32),
                pltpu.VMEM((nb, 128), F32),
                dma((n_sp,)), dma((n_sp,)), dma((n_sp,)), dma((n_sp,)),
                dma((slots, 2)), dma((slots, 2)),
                dma((ITERS,)), dma((ITERS,)),
                dma((ITERS, n_tm)), dma((ITERS, n_tm)),
            ],
            compiler_params=pltpu.CompilerParams(collective_id=0, has_side_effects=True),
        )(
            init_state, guess, source, remap.reshape(1, nb), neighbors, block_class.reshape(1, nb),
            step_number.reshape(1, CLASSES), inverse.reshape(CLASSES * COARSE, COARSE),
            cstep.reshape(CLASSES * COARSE, COARSE),
        )

    placed = (
        P("space", None), P("tm", "space", None), P("tm", None, "space", None), P("space"),
        P("space", None), P("space"), P(), P(), P(),
    )
    return jax.shard_map(
        body, mesh=mesh, in_specs=placed,
        out_specs=(P("tm", "space", None), P("tm", "space", None)), check_vma=False,
    )
```

```python
import functools

import jax
import jax.numpy as jnp
from jax import lax
from jax.experimental import pallas as pl
from jax.experimental.pallas import tpu as pltpu
from jax.sharding import PartitionSpec as P

CELLS = 512
COARSE = 64
CLASSES = 4
ITERS = 2
DAMP = 0.8
MESH = pl.DeviceIdType.MESH
F32 = jnp.float32
BF16 = jnp.bfloat16


def split(value):
    high = value.astype(BF16)
    return high, (value - high.astype(F32)).astype(BF16)


def dot(left, right):
    return jnp.dot(left, right, preferred_element_type=F32)


def roll(value, shift):
    shift = shift % 128
    return value if shift == 0 else pltpu.roll(value, shift, 1)


def iota(shape, dim):
    return lax.broadcasted_iota(jnp.int32, shape, dim)


def kernel(
    n_tm, n_sp, bk,
    init_ref, guess_ref, source_ref, remap_ref, nb_ref, class_ref, step_ref, inv_ref, cstep_ref,
    c_ref, f_ref,
    gb, ib, gr, br, hs, hr, st, hsrc, hand, cs, cr,
    ohl, ohn, oh4, oh5, oh4t, oh5t, rm, pm, mi, ms, xs, ws, bs, zs, ps, scale, near,
    gs_sem, gr_sem, ps_sem, is_sem, br_sem, hs_sem, hr_sem, ts_sem, tr_sem, cs_sem, cr_sem,
):
    k = lax.axis_index("tm")
    s = lax.axis_index("space")
    nb = init_ref.shape[0]
    rows = n_sp * bk
    bits = nb.bit_length() - 1
    setup = ITERS * 4

    hr[...] = jnp.zeros_like(hr)
    barrier = pltpu.get_barrier_semaphore()
    for off in range(1, n_sp):
        pl.semaphore_signal(barrier, inc=1, device_id=(k, lax.rem(s + off, n_sp)), device_id_type=MESH)
    for off in range(1, n_tm):
        pl.semaphore_signal(barrier, inc=1, device_id=(lax.rem(k + off, n_tm), s), device_id_type=MESH)

    @pl.when(k < n_tm - 1)
    def _():
        for off in range(1, n_sp):
            pl.semaphore_signal(barrier, inc=1, device_id=(k + 1, lax.rem(s + off, n_sp)), device_id_type=MESH)

    @pl.when(k > 0)
    def _():
        for off in range(1, n_sp):
            pl.semaphore_signal(barrier, inc=1, device_id=(k - 1, lax.rem(s + off, n_sp)), device_id_type=MESH)

    eye = iota((nb, nb), 0) == iota((nb, nb), 1)

    def column(row):
        return jnp.sum(jnp.where(eye, row, 0.0), axis=1, keepdims=True)

    remap_row = remap_ref[...]
    target_row = lax.shift_right_logical(remap_row, bits)
    slot_row = (remap_row - lax.shift_left(target_row, bits)).astype(F32)
    target_f = target_row.astype(F32)
    same = (column(target_f) == target_f) & (iota((nb, nb), 0) < iota((nb, nb), 1))
    pos_row = jnp.sum(jnp.where(same, 1.0, 0.0), axis=0, keepdims=True)
    send_row = target_f * float(bk) + pos_row
    chosen = iota((rows, nb), 0).astype(F32) == send_row
    send_mat = jnp.where(chosen, 1.0, 0.0)
    slot_col = jnp.sum(jnp.where(chosen, slot_row + 1.0, 0.0), axis=1, keepdims=True) - 1.0
    send_mat = jnp.concatenate([send_mat, send_mat], axis=1).astype(BF16)

    def bucketed(value):
        return dot(send_mat, jnp.concatenate(split(value), axis=0)).reshape(n_sp, bk, CELLS)

    slot_tile = jnp.broadcast_to(slot_col, (rows, 128)).reshape(n_sp, bk, 128)
    gb[:, :, :CELLS] = bucketed(guess_ref[0])
    gb[:, :, CELLS:] = slot_tile

    @pl.when(k == 0)
    def _():
        ib[:, :, :CELLS] = bucketed(init_ref[...])
        ib[:, :, CELLS:] = slot_tile

    sides = jnp.minimum(k, 1) + jnp.minimum(n_tm - 1 - k, 1)
    pl.semaphore_wait(barrier, (n_sp - 1) * (1 + sides) + n_tm - 1)

    def spread_copy(src, ssem, off, col):
        to = lax.rem(s + off, n_sp)
        return pltpu.make_async_remote_copy(
            src_ref=src.at[to], dst_ref=br.at[s], send_sem=ssem.at[off], recv_sem=br_sem.at[s],
            device_id=(col, to), device_id_type=MESH)

    def own_copy(off):
        to = lax.rem(s + off, n_sp)
        return pltpu.make_async_remote_copy(
            src_ref=gb.at[to, :, pl.ds(0, CELLS)], dst_ref=gr.at[s], send_sem=gs_sem.at[off],
            recv_sem=gr_sem.at[s], device_id=(k, to), device_id_type=MESH)

    def spread_landed(off):
        origin = lax.rem(s + off, n_sp)
        pltpu.make_async_remote_copy(
            src_ref=gb.at[origin], dst_ref=br.at[origin], send_sem=ps_sem.at[off],
            recv_sem=br_sem.at[origin], device_id=(lax.rem(k + 1, n_tm), origin),
            device_id_type=MESH).wait_recv()

    def own_landed(off):
        origin = lax.rem(s + off, n_sp)
        pltpu.make_async_remote_copy(
            src_ref=gb.at[origin, :, pl.ds(0, CELLS)], dst_ref=gr.at[origin],
            send_sem=gs_sem.at[off], recv_sem=gr_sem.at[origin], device_id=(k, origin),
            device_id_type=MESH).wait_recv()

    @pl.when(k == 0)
    def _():
        for off in range(1, n_sp):
            spread_copy(ib, is_sem, off, k).start()
        br[s] = ib[s]

    @pl.when(k < n_tm - 1)
    def _():
        for off in range(n_sp):
            spread_copy(gb, ps_sem, off, lax.rem(k + 1, n_tm)).start()

    class_col = column(class_ref[...].astype(F32))
    diffusion = jnp.zeros((nb, 1), F32)
    for cl in range(CLASSES):
        diffusion = diffusion + jnp.where(class_col == float(cl), step_ref[:, cl:cl + 1], 0.0)
    dif = jnp.broadcast_to(diffusion, (nb, 128))
    scale[0] = DAMP * dif / (1.0 + 6.0 * dif)
    scale[1] = DAMP / (1.0 + 6.0 * dif)
    scale[2] = (1.0 + 6.0 * dif) / DAMP
    lane = iota((nb, 128), 1)
    table = jnp.where(lane == 4, dif, -1.0)
    for face in range(4):
        table = jnp.where(lane == face, (nb_ref[:, face:face + 1] - s * nb).astype(F32), table)
    hs[setup, 0] = table
    hs[setup, 1] = table

    def halo_up(slot):
        return pltpu.make_async_remote_copy(
            src_ref=hs.at[slot, 0], dst_ref=hr.at[slot, 0], send_sem=hs_sem.at[slot, 0],
            recv_sem=hr_sem.at[slot, 0], device_id=(k, lax.rem(s + 1, n_sp)), device_id_type=MESH)

    def halo_down(slot):
        return pltpu.make_async_remote_copy(
            src_ref=hs.at[slot, 1], dst_ref=hr.at[slot, 1], send_sem=hs_sem.at[slot, 1],
            recv_sem=hr_sem.at[slot, 1], device_id=(k, lax.rem(s + n_sp - 1, n_sp)), device_id_type=MESH)

    def exchange(slot):
        @pl.when(s < n_sp - 1)
        def _():
            halo_up(slot).start()

        @pl.when(s > 0)
        def _():
            halo_down(slot).start()

    def exchanged(slot):
        @pl.when(s > 0)
        def _():
            halo_up(slot).wait_recv()

        @pl.when(s < n_sp - 1)
        def _():
            halo_down(slot).wait_recv()

    exchange(setup)
    for off in range(1, n_sp):
        own_copy(off).start()
    gr[s] = gb[s, :, :CELLS]

    lane_nb = iota((nb, nb), 1)
    for face in range(6):
        shift = s * nb + (0 if face < 4 else (-nb if face == 4 else nb))
        ids = nb_ref[:, face:face + 1]
        hot = jnp.where((ids - shift == lane_nb) & (ids >= 0), 1.0, 0.0)
        if face >= 4:
            turned = hot.T
            turned = jnp.concatenate([turned, turned], axis=1).astype(BF16)
            (oh4t if face == 4 else oh5t)[...] = turned
        hot = jnp.concatenate([hot, hot], axis=1).astype(BF16)
        if face < 4:
            ohl[face * nb:(face + 1) * nb] = hot
        elif face == 4:
            oh4[...] = hot
        else:
            oh5[...] = hot

    def parent(cell):
        return (lax.shift_right_logical(cell, 7) * 16
                + (lax.shift_right_logical(cell, 4) & 3) * 4
                + lax.shift_right_logical(cell & 7, 1))

    rm[...] = jnp.where(parent(iota((CELLS, 128), 0)) == iota((CELLS, 128), 1), 0.125, 0.0).astype(BF16)
    pm[...] = jnp.where(parent(iota((128, CELLS), 1)) == (iota((128, CELLS), 0) & 63), 1.0, 0.0).astype(BF16)
    for src, dst in ((inv_ref, mi), (cstep_ref, ms)):
        high, low = split(src[...].T)
        dst[...] = jnp.concatenate([high, high, low, jnp.zeros_like(low)], axis=0)

    zz = lane & 7
    yy = lax.shift_right_logical(lane, 3) & 7
    left = lane < 64

    def classes(coarse, mat):
        high = coarse.astype(BF16).astype(F32)
        both = high + roll(coarse - high, 64)
        product = dot(jnp.concatenate([both, high], axis=1).astype(BF16), mat[...])
        low_c = jnp.where(left, 0.0, 1.0)
        picked = (jnp.where(class_col == low_c, product[:, :128], 0.0)
                  + jnp.where(class_col == low_c + 2.0, product[:, 128:], 0.0))
        return jnp.where(left, picked + roll(picked, 64), 0.0)

    def prolong(coarse):
        high = coarse.astype(BF16).astype(F32)
        return dot((high + roll(coarse - high, 64)).astype(BF16), pm[...])

    def restrict(value):
        both = dot(jnp.concatenate(split(value), axis=0), rm[...])
        return both[:nb] + both[nb:]

    def tiles_of(value):
        return [value[:, 128 * j:128 * j + 128] for j in range(4)]

    def gathered(hot, value):
        return dot(hot, jnp.concatenate(split(value), axis=0))

    def planes(tiles):
        top = bottom = jnp.zeros((nb, 128), F32)
        for j in range(4):
            top = jnp.where(zz == j, roll(tiles[j], j - 7), top)
            top = jnp.where(zz == 4 + j, roll(tiles[j], j - 2), top)
            bottom = jnp.where(zz == j, roll(tiles[j], j), bottom)
            bottom = jnp.where(zz == 4 + j, roll(tiles[j], j + 3), bottom)
        return top, bottom

    def plane_step(plane, driven, side, cross):
        w = gathered(ohn[side], plane)
        turned = roll(plane, 64)
        total = turned + jnp.where(
            left, jnp.where(zz == 0, roll(w[:nb], -67), roll(turned, 1)),
            jnp.where(zz == 3, roll(w[nb:2 * nb], 67), roll(turned, -1)))
        total = total + jnp.where(yy == 0, roll(w[2 * nb:3 * nb], -56), roll(plane, 8))
        total = total + jnp.where(yy == 7, roll(w[3 * nb:], 56), roll(plane, -8))
        total = total + roll(plane, -4) + cross
        return (1.0 - DAMP) * plane + driven + near[side] * total

    def inside(tiles):
        xface = jnp.where(left, roll(tiles[3], 64), roll(tiles[0], 64))
        yface = jnp.zeros((nb, 128), F32)
        for j in range(4):
            yface = jnp.where(yy == j, roll(tiles[j], 8 * j - 56), yface)
            yface = jnp.where(yy == 4 + j, roll(tiles[j], 32 + 8 * j), yface)
        ghosts = gathered(ohl[...], jnp.concatenate([xface, yface], axis=1))
        turned = [roll(tile, 64) for tile in tiles]
        turned = [ghosts[:nb, :128]] + turned + [ghosts[nb:2 * nb, :128]]
        g2 = ghosts[2 * nb:3 * nb, 128:]
        g3 = ghosts[3 * nb:, 128:]
        sums = []
        for j in range(4):
            total = turned[j + 1] + jnp.where(left, turned[j], turned[j + 2])
            total = total + jnp.where(yy == 0, roll(g2, -8 * j), roll(tiles[j], 8))
            total = total + jnp.where(yy == 7, roll(g3, 24 - 8 * j), roll(tiles[j], -8))
            total = total + jnp.where(zz == 0, 0.0, roll(tiles[j], 1))
            total = total + jnp.where(zz == 7, 0.0, roll(tiles[j], -1))
            sums.append(total)
        return sums

    def with_ends(sums, below, above):
        g4 = gathered(oh4[...], below)
        g5 = gathered(oh5[...], above)
        return [
            sums[j] + jnp.where(zz == 0, roll(g4, -j), 0.0) + jnp.where(zz == 7, roll(g5, 7 - j), 0.0)
            for j in range(4)
        ]

    def swept(tiles, driven, sums):
        return [(1.0 - DAMP) * tiles[j] + driven[j] + scale[0] * sums[j] for j in range(4)]

    def vcycle(base):
        driven = tiles_of(ws[...])
        for stage in range(2):
            slot = base + stage
            tiles = driven if stage == 0 else tiles_of(xs[...])
            top, bottom = planes(tiles)
            hs[slot, 0] = top
            hs[slot, 1] = bottom
            exchange(slot)
            sums = inside(tiles)
            up_cross = gathered(oh4t[...], bottom)
            down_cross = gathered(oh5t[...], top)
            exchanged(slot)
            below, above = hr[slot, 0], hr[slot, 1]
            tiles = swept(tiles, driven, with_ends(sums, below, above))
            below = plane_step(below, hr[base, 0], 0, up_cross)
            above = plane_step(above, hr[base, 1], 1, down_cross)
            sums = with_ends(inside(tiles), below, above)
            if stage == 0:
                rest = jnp.concatenate(
                    [driven[j] - DAMP * tiles[j] + scale[0] * sums[j] for j in range(4)], axis=1)
                fix = prolong(classes(scale[2] * restrict(rest), mi))
                xs[...] = jnp.concatenate(tiles, axis=1) + fix
            else:
                xs[...] = jnp.concatenate(swept(tiles, driven, sums), axis=1)

    def drive(value):
        ws[...] = value * jnp.concatenate([scale[1]] * 4, axis=1)

    exchanged(setup)
    for side in range(2):
        table = hr[setup, side]
        far = table[:, 4:5]
        near[side] = jnp.broadcast_to(DAMP * far / (1.0 + 6.0 * far), (nb, 128))
        for face in range(4):
            hot = jnp.where(table[:, face:face + 1] == lane_nb.astype(F32), 1.0, 0.0)
            ohn[side, face * nb:(face + 1) * nb] = jnp.concatenate([hot, hot], axis=1).astype(BF16)

    for off in range(1, n_sp):
        spread_landed(off)

    @pl.when(k > 0)
    def _():
        spread_landed(0)

    arrived = br[...].reshape(rows, CELLS + 128)
    slots = arrived[:, CELLS:CELLS + nb]
    take = jnp.where(slots == iota((rows, nb), 1).astype(F32), 1.0, 0.0).T.astype(BF16)

    def settled(value):
        high, low = split(value)
        return dot(take, high) + dot(take, low)

    bs[...] = settled(arrived[:, :CELLS])

    def hand_copy(it):
        return pltpu.make_async_remote_copy(
            src_ref=hsrc.at[it], dst_ref=hand.at[it], send_sem=ts_sem.at[it], recv_sem=tr_sem.at[it],
            device_id=(lax.rem(k + 1, n_tm), s), device_id_type=MESH)

    def coarse_copy(it, off):
        return pltpu.make_async_remote_copy(
            src_ref=cs.at[it], dst_ref=cr.at[it, k], send_sem=cs_sem.at[it, off],
            recv_sem=cr_sem.at[it, k], device_id=(lax.rem(k + off, n_tm), s), device_id_type=MESH)

    def coarse_landed(it, origin):
        pltpu.make_async_remote_copy(
            src_ref=cs.at[it], dst_ref=cr.at[it, origin], send_sem=cs_sem.at[it, 0],
            recv_sem=cr_sem.at[it, origin], device_id=(lax.rem(k + 1, n_tm), s),
            device_id_type=MESH).wait_recv()

    def iteration(it, carry):
        drive(bs[...] + source_ref[0, 0])

        def one(v, c):
            vcycle((it * 2 + v) * 2)

            @pl.when(v == 0)
            def _():
                f_ref[0] = xs[...]
                drive(xs[...] + source_ref[0, 1])
            return c

        lax.fori_loop(0, 2, one, 0)

        @pl.when(it == 0)
        def _():
            for off in range(1, n_sp):
                own_landed(off)
            st[0] = settled(gr[...].reshape(rows, CELLS))

        residual = xs[...] - st[it]
        cs[it] = restrict(residual)
        for off in range(1, n_tm):
            @pl.when(k + off < n_tm)
            def _():
                coarse_copy(it, off).start()

        @pl.when((k < n_tm - 1) & (it < ITERS - 1))
        def _():
            hsrc[it] = xs[...]
            hand_copy(it).start()

        zs[...] = jnp.zeros_like(zs)
        ps[...] = jnp.zeros_like(ps)
        for j in range(n_tm - 1):
            @pl.when(j < k)
            def _():
                coarse_landed(it, j)
                pushed = classes(zs[...], ms)
                ps[...] = pushed
                zs[...] = pushed + cr[it, j]
        st[it + 1] = st[it] + (prolong(classes(zs[...], ms)) + residual)

        @pl.when((k > 0) & (it < ITERS - 1))
        def _():
            hand_copy(it).wait_recv()
            bs[...] = hand[it] + prolong(ps[...])
        return carry

    lax.fori_loop(0, ITERS, iteration, 0)
    c_ref[0] = st[ITERS]

    for off in range(1, n_sp):
        own_copy(off).wait_send()

    @pl.when(k == 0)
    def _():
        for off in range(1, n_sp):
            spread_copy(ib, is_sem, off, k).wait_send()

    @pl.when(k < n_tm - 1)
    def _():
        for off in range(n_sp):
            spread_copy(gb, ps_sem, off, lax.rem(k + 1, n_tm)).wait_send()

    def drain(slot, carry):
        @pl.when(s < n_sp - 1)
        def _():
            halo_up(slot).wait_send()

        @pl.when(s > 0)
        def _():
            halo_down(slot).wait_send()
        return carry

    lax.fori_loop(0, setup + 1, drain, 0)
    for it in range(ITERS):
        if it < ITERS - 1:
            @pl.when(k < n_tm - 1)
            def _():
                hand_copy(it).wait_send()
        for off in range(1, n_tm):
            @pl.when(k + off < n_tm)
            def _():
                coarse_copy(it, off).wait_send()


def solution(mesh):
    n_tm, n_sp = mesh.shape["tm"], mesh.shape["space"]

    def body(init_state, guess, source, remap, neighbors, block_class, step_number, inverse, cstep):
        nb = init_state.shape[0]
        bk = -(-(2 * nb // n_sp) // 8) * 8
        slots = ITERS * 4 + 1
        dma = pltpu.SemaphoreType.DMA
        out = jax.ShapeDtypeStruct((1, nb, CELLS), F32)
        return pl.pallas_call(
            functools.partial(kernel, n_tm, n_sp, bk),
            name="mgrit",
            out_shape=(out, out),
            in_specs=[pl.BlockSpec(memory_space=pltpu.VMEM)] * 9,
            out_specs=[pl.BlockSpec(memory_space=pltpu.VMEM)] * 2,
            scratch_shapes=[
                pltpu.VMEM((n_sp, bk, CELLS + 128), F32),
                pltpu.VMEM((n_sp, bk, CELLS + 128), F32),
                pltpu.VMEM((n_sp, bk, CELLS), F32),
                pltpu.VMEM((n_sp, bk, CELLS + 128), F32),
                pltpu.VMEM((slots, 2, nb, 128), F32),
                pltpu.VMEM((slots, 2, nb, 128), F32),
                pltpu.VMEM((ITERS + 1, nb, CELLS), F32),
                pltpu.VMEM((ITERS, nb, CELLS), F32),
                pltpu.VMEM((ITERS, nb, CELLS), F32),
                pltpu.VMEM((ITERS, nb, 128), F32),
                pltpu.VMEM((ITERS, n_tm, nb, 128), F32),
                pltpu.VMEM((4 * nb, 2 * nb), BF16),
                pltpu.VMEM((2, 4 * nb, 2 * nb), BF16),
                pltpu.VMEM((nb, 2 * nb), BF16),
                pltpu.VMEM((nb, 2 * nb), BF16),
                pltpu.VMEM((nb, 2 * nb), BF16),
                pltpu.VMEM((nb, 2 * nb), BF16),
                pltpu.VMEM((CELLS, 128), BF16),
                pltpu.VMEM((128, CELLS), BF16),
                pltpu.VMEM((4 * COARSE, CLASSES * COARSE), BF16),
                pltpu.VMEM((4 * COARSE, CLASSES * COARSE), BF16),
                pltpu.VMEM((nb, CELLS), F32),
                pltpu.VMEM((nb, CELLS), F32),
                pltpu.VMEM((nb, CELLS), F32),
                pltpu.VMEM((nb, 128), F32),
                pltpu.VMEM((nb, 128), F32),
                pltpu.VMEM((3, nb, 128), F32),
                pltpu.VMEM((2, nb, 128), F32),
                dma((n_sp,)), dma((n_sp,)), dma((n_sp,)), dma((n_sp,)), dma((n_sp,)),
                dma((slots, 2)), dma((slots, 2)),
                dma((ITERS,)), dma((ITERS,)),
                dma((ITERS, n_tm)), dma((ITERS, n_tm)),
            ],
            compiler_params=pltpu.CompilerParams(collective_id=0, has_side_effects=True),
        )(
            init_state, guess, source, remap.reshape(1, nb), neighbors, block_class.reshape(1, nb),
            step_number.reshape(1, CLASSES), inverse.reshape(CLASSES * COARSE, COARSE),
            cstep.reshape(CLASSES * COARSE, COARSE),
        )

    placed = (
        P("space", None), P("tm", "space", None), P("tm", None, "space", None), P("space"),
        P("space", None), P("space"), P(), P(), P(),
    )
    return jax.shard_map(
        body, mesh=mesh, in_specs=placed,
        out_specs=(P("tm", "space", None), P("tm", "space", None)), check_vma=False,
    )
```

```python
import functools

import jax
import jax.numpy as jnp
from jax import lax
from jax.experimental import pallas as pl
from jax.experimental.pallas import tpu as pltpu
from jax.sharding import PartitionSpec as P

CELLS = 512
COARSE = 64
CLASSES = 4
ITERS = 2
DAMP = 0.8
MESH = pl.DeviceIdType.MESH
F32 = jnp.float32
BF16 = jnp.bfloat16


def split(value):
    high = value.astype(BF16)
    return high, (value - high.astype(F32)).astype(BF16)


def dot(left, right):
    return jnp.dot(left, right, preferred_element_type=F32)


def roll(value, shift):
    shift = shift % 128
    return value if shift == 0 else pltpu.roll(value, shift, 1)


def iota(shape, dim):
    return lax.broadcasted_iota(jnp.int32, shape, dim)


def kernel(
    n_tm, n_sp, bk,
    init_ref, guess_ref, source_ref, remap_ref, nb_ref, class_ref, step_ref, inv_ref, cstep_ref,
    c_ref, f_ref,
    gb, ib, gr, br, hs, hr, st, hsrc, hand, cs, cr,
    ohl, ohn, oh4, oh5, oh4t, oh5t, rm, pm, mi, ms, xs, ws, bs, zs, ps, scale, near,
    slots_out, slots_in, so_sem, si_sem,
    gs_sem, gr_sem, ps_sem, is_sem, br_sem, hs_sem, hr_sem, ts_sem, tr_sem, cs_sem, cr_sem,
):
    k = lax.axis_index("tm")
    s = lax.axis_index("space")
    nb = init_ref.shape[0]
    rows = n_sp * bk
    bits = nb.bit_length() - 1
    setup = ITERS * 4

    hr[...] = jnp.zeros_like(hr)
    barrier = pltpu.get_barrier_semaphore()
    for off in range(1, n_sp):
        pl.semaphore_signal(barrier, inc=1, device_id=(k, lax.rem(s + off, n_sp)), device_id_type=MESH)
    for off in range(1, n_tm):
        pl.semaphore_signal(barrier, inc=1, device_id=(lax.rem(k + off, n_tm), s), device_id_type=MESH)

    @pl.when(k < n_tm - 1)
    def _():
        for off in range(1, n_sp):
            pl.semaphore_signal(barrier, inc=1, device_id=(k + 1, lax.rem(s + off, n_sp)), device_id_type=MESH)

    @pl.when(k > 0)
    def _():
        for off in range(1, n_sp):
            pl.semaphore_signal(barrier, inc=1, device_id=(k - 1, lax.rem(s + off, n_sp)), device_id_type=MESH)

    eye = iota((nb, nb), 0) == iota((nb, nb), 1)

    def column(row):
        return jnp.sum(jnp.where(eye, row, 0.0), axis=1, keepdims=True)

    remap_row = remap_ref[...]
    target_row = lax.shift_right_logical(remap_row, bits)
    slot_row = (remap_row - lax.shift_left(target_row, bits)).astype(F32)
    target_f = target_row.astype(F32)
    same = (column(target_f) == target_f) & (iota((nb, nb), 0) < iota((nb, nb), 1))
    pos_row = jnp.sum(jnp.where(same, 1.0, 0.0), axis=0, keepdims=True)
    send_row = target_f * float(bk) + pos_row
    chosen = iota((rows, nb), 0).astype(F32) == send_row
    send_mat = jnp.where(chosen, 1.0, 0.0)
    slot_col = jnp.sum(jnp.where(chosen, slot_row + 1.0, 0.0), axis=1, keepdims=True) - 1.0
    send_mat = jnp.concatenate([send_mat, send_mat], axis=1).astype(BF16)

    def bucketed(value):
        return dot(send_mat, jnp.concatenate(split(value), axis=0)).reshape(n_sp, bk, CELLS)

    spot = iota((n_sp, bk, 128), 1) == iota((n_sp, bk, 128), 2)
    slot_wide = jnp.broadcast_to(slot_col, (rows, 128)).reshape(n_sp, bk, 128)
    slot_lanes = jnp.sum(jnp.where(spot, slot_wide, 0.0), axis=1, keepdims=True)
    slots_out[...] = jnp.broadcast_to(slot_lanes, (n_sp, 8, 128))
    gb[...] = bucketed(guess_ref[0])

    @pl.when(k == 0)
    def _():
        ib[...] = bucketed(init_ref[...])

    sides = jnp.minimum(k, 1) + jnp.minimum(n_tm - 1 - k, 1)
    pl.semaphore_wait(barrier, (n_sp - 1) * (1 + sides) + n_tm - 1)

    def spread_copy(src, ssem, off, col):
        to = lax.rem(s + off, n_sp)
        return pltpu.make_async_remote_copy(
            src_ref=src.at[to], dst_ref=br.at[s], send_sem=ssem.at[off], recv_sem=br_sem.at[s],
            device_id=(col, to), device_id_type=MESH)

    def own_copy(off):
        to = lax.rem(s + off, n_sp)
        return pltpu.make_async_remote_copy(
            src_ref=gb.at[to], dst_ref=gr.at[s], send_sem=gs_sem.at[off],
            recv_sem=gr_sem.at[s], device_id=(k, to), device_id_type=MESH)

    def spread_landed(off):
        origin = lax.rem(s + off, n_sp)
        pltpu.make_async_remote_copy(
            src_ref=gb.at[origin], dst_ref=br.at[origin], send_sem=ps_sem.at[off],
            recv_sem=br_sem.at[origin], device_id=(lax.rem(k + 1, n_tm), origin),
            device_id_type=MESH).wait_recv()

    def own_landed(off):
        origin = lax.rem(s + off, n_sp)
        pltpu.make_async_remote_copy(
            src_ref=gb.at[origin], dst_ref=gr.at[origin],
            send_sem=gs_sem.at[off], recv_sem=gr_sem.at[origin], device_id=(k, origin),
            device_id_type=MESH).wait_recv()

    def slots_copy(off):
        to = lax.rem(s + off, n_sp)
        return pltpu.make_async_remote_copy(
            src_ref=slots_out.at[to], dst_ref=slots_in.at[s], send_sem=so_sem.at[off],
            recv_sem=si_sem.at[s], device_id=(k, to), device_id_type=MESH)

    def slots_landed(off):
        origin = lax.rem(s + off, n_sp)
        pltpu.make_async_remote_copy(
            src_ref=slots_out.at[origin], dst_ref=slots_in.at[origin], send_sem=so_sem.at[off],
            recv_sem=si_sem.at[origin], device_id=(k, origin), device_id_type=MESH).wait_recv()

    for off in range(1, n_sp):
        slots_copy(off).start()
    slots_in[s] = slots_out[s]

    @pl.when(k == 0)
    def _():
        for off in range(1, n_sp):
            spread_copy(ib, is_sem, off, k).start()
        br[s] = ib[s]

    @pl.when(k < n_tm - 1)
    def _():
        for off in range(n_sp):
            spread_copy(gb, ps_sem, off, lax.rem(k + 1, n_tm)).start()

    class_col = column(class_ref[...].astype(F32))
    diffusion = jnp.zeros((nb, 1), F32)
    for cl in range(CLASSES):
        diffusion = diffusion + jnp.where(class_col == float(cl), step_ref[:, cl:cl + 1], 0.0)
    dif = jnp.broadcast_to(diffusion, (nb, 128))
    scale[0] = DAMP * dif / (1.0 + 6.0 * dif)
    scale[1] = DAMP / (1.0 + 6.0 * dif)
    scale[2] = (1.0 + 6.0 * dif) / DAMP
    lane = iota((nb, 128), 1)
    table = jnp.where(lane == 4, dif, -1.0)
    for face in range(4):
        table = jnp.where(lane == face, (nb_ref[:, face:face + 1] - s * nb).astype(F32), table)
    hs[setup, 0] = table
    hs[setup, 1] = table

    def halo_up(slot):
        return pltpu.make_async_remote_copy(
            src_ref=hs.at[slot, 0], dst_ref=hr.at[slot, 0], send_sem=hs_sem.at[slot, 0],
            recv_sem=hr_sem.at[slot, 0], device_id=(k, lax.rem(s + 1, n_sp)), device_id_type=MESH)

    def halo_down(slot):
        return pltpu.make_async_remote_copy(
            src_ref=hs.at[slot, 1], dst_ref=hr.at[slot, 1], send_sem=hs_sem.at[slot, 1],
            recv_sem=hr_sem.at[slot, 1], device_id=(k, lax.rem(s + n_sp - 1, n_sp)), device_id_type=MESH)

    def exchange(slot):
        @pl.when(s < n_sp - 1)
        def _():
            halo_up(slot).start()

        @pl.when(s > 0)
        def _():
            halo_down(slot).start()

    def exchanged(slot):
        @pl.when(s > 0)
        def _():
            halo_up(slot).wait_recv()

        @pl.when(s < n_sp - 1)
        def _():
            halo_down(slot).wait_recv()

    exchange(setup)
    gr[s] = gb[s]

    lane_nb = iota((nb, nb), 1)
    for face in range(6):
        shift = s * nb + (0 if face < 4 else (-nb if face == 4 else nb))
        ids = nb_ref[:, face:face + 1]
        hot = jnp.where((ids - shift == lane_nb) & (ids >= 0), 1.0, 0.0)
        if face >= 4:
            turned = hot.T
            turned = jnp.concatenate([turned, turned], axis=1).astype(BF16)
            (oh4t if face == 4 else oh5t)[...] = turned
        hot = jnp.concatenate([hot, hot], axis=1).astype(BF16)
        if face < 4:
            ohl[face * nb:(face + 1) * nb] = hot
        elif face == 4:
            oh4[...] = hot
        else:
            oh5[...] = hot

    def parent(cell):
        return (lax.shift_right_logical(cell, 7) * 16
                + (lax.shift_right_logical(cell, 4) & 3) * 4
                + lax.shift_right_logical(cell & 7, 1))

    rm[...] = jnp.where(parent(iota((CELLS, 128), 0)) == iota((CELLS, 128), 1), 0.125, 0.0).astype(BF16)
    pm[...] = jnp.where(parent(iota((128, CELLS), 1)) == (iota((128, CELLS), 0) & 63), 1.0, 0.0).astype(BF16)
    for src, dst in ((inv_ref, mi), (cstep_ref, ms)):
        high, low = split(src[...].T)
        dst[...] = jnp.concatenate([high, high, low, jnp.zeros_like(low)], axis=0)

    zz = lane & 7
    yy = lax.shift_right_logical(lane, 3) & 7
    left = lane < 64

    def classes(coarse, mat):
        high = coarse.astype(BF16).astype(F32)
        both = high + roll(coarse - high, 64)
        product = dot(jnp.concatenate([both, high], axis=1).astype(BF16), mat[...])
        low_c = jnp.where(left, 0.0, 1.0)
        picked = (jnp.where(class_col == low_c, product[:, :128], 0.0)
                  + jnp.where(class_col == low_c + 2.0, product[:, 128:], 0.0))
        return jnp.where(left, picked + roll(picked, 64), 0.0)

    def prolong(coarse):
        high = coarse.astype(BF16).astype(F32)
        return dot((high + roll(coarse - high, 64)).astype(BF16), pm[...])

    def restrict(value):
        both = dot(jnp.concatenate(split(value), axis=0), rm[...])
        return both[:nb] + both[nb:]

    def tiles_of(value):
        return [value[:, 128 * j:128 * j + 128] for j in range(4)]

    def gathered(hot, value):
        return dot(hot, jnp.concatenate(split(value), axis=0))

    def planes(tiles):
        top = bottom = jnp.zeros((nb, 128), F32)
        for j in range(4):
            top = jnp.where(zz == j, roll(tiles[j], j - 7), top)
            top = jnp.where(zz == 4 + j, roll(tiles[j], j - 2), top)
            bottom = jnp.where(zz == j, roll(tiles[j], j), bottom)
            bottom = jnp.where(zz == 4 + j, roll(tiles[j], j + 3), bottom)
        return top, bottom

    def plane_step(plane, driven, side, cross):
        w = gathered(ohn[side], plane)
        turned = roll(plane, 64)
        total = turned + jnp.where(
            left, jnp.where(zz == 0, roll(w[:nb], -67), roll(turned, 1)),
            jnp.where(zz == 3, roll(w[nb:2 * nb], 67), roll(turned, -1)))
        total = total + jnp.where(yy == 0, roll(w[2 * nb:3 * nb], -56), roll(plane, 8))
        total = total + jnp.where(yy == 7, roll(w[3 * nb:], 56), roll(plane, -8))
        total = total + roll(plane, -4) + cross
        return (1.0 - DAMP) * plane + driven + near[side] * total

    def inside(tiles):
        xface = jnp.where(left, roll(tiles[3], 64), roll(tiles[0], 64))
        yface = jnp.zeros((nb, 128), F32)
        for j in range(4):
            yface = jnp.where(yy == j, roll(tiles[j], 8 * j - 56), yface)
            yface = jnp.where(yy == 4 + j, roll(tiles[j], 32 + 8 * j), yface)
        ghosts = gathered(ohl[...], jnp.concatenate([xface, yface], axis=1))
        turned = [roll(tile, 64) for tile in tiles]
        turned = [ghosts[:nb, :128]] + turned + [ghosts[nb:2 * nb, :128]]
        g2 = ghosts[2 * nb:3 * nb, 128:]
        g3 = ghosts[3 * nb:, 128:]
        sums = []
        for j in range(4):
            total = turned[j + 1] + jnp.where(left, turned[j], turned[j + 2])
            total = total + jnp.where(yy == 0, roll(g2, -8 * j), roll(tiles[j], 8))
            total = total + jnp.where(yy == 7, roll(g3, 24 - 8 * j), roll(tiles[j], -8))
            total = total + jnp.where(zz == 0, 0.0, roll(tiles[j], 1))
            total = total + jnp.where(zz == 7, 0.0, roll(tiles[j], -1))
            sums.append(total)
        return sums

    def with_ends(sums, below, above):
        g4 = gathered(oh4[...], below)
        g5 = gathered(oh5[...], above)
        return [
            sums[j] + jnp.where(zz == 0, roll(g4, -j), 0.0) + jnp.where(zz == 7, roll(g5, 7 - j), 0.0)
            for j in range(4)
        ]

    def swept(tiles, driven, sums):
        return [(1.0 - DAMP) * tiles[j] + driven[j] + scale[0] * sums[j] for j in range(4)]

    def vcycle(base):
        driven = tiles_of(ws[...])
        for stage in range(2):
            slot = base + stage
            tiles = driven if stage == 0 else tiles_of(xs[...])
            top, bottom = planes(tiles)
            hs[slot, 0] = top
            hs[slot, 1] = bottom
            exchange(slot)
            for off in range(1, n_sp):
                turn = (off - 1) * 4 // (n_sp - 1)

                @pl.when((k == n_tm - 1) & (slot == turn))
                def _():
                    own_copy(off).start()
            sums = inside(tiles)
            up_cross = gathered(oh4t[...], bottom)
            down_cross = gathered(oh5t[...], top)
            exchanged(slot)
            below, above = hr[slot, 0], hr[slot, 1]
            tiles = swept(tiles, driven, with_ends(sums, below, above))
            below = plane_step(below, hr[base, 0], 0, up_cross)
            above = plane_step(above, hr[base, 1], 1, down_cross)
            sums = with_ends(inside(tiles), below, above)
            if stage == 0:
                rest = jnp.concatenate(
                    [driven[j] - DAMP * tiles[j] + scale[0] * sums[j] for j in range(4)], axis=1)
                fix = prolong(classes(scale[2] * restrict(rest), mi))
                xs[...] = jnp.concatenate(tiles, axis=1) + fix
            else:
                xs[...] = jnp.concatenate(swept(tiles, driven, sums), axis=1)

    def drive(value):
        ws[...] = value * jnp.concatenate([scale[1]] * 4, axis=1)

    exchanged(setup)
    for side in range(2):
        table = hr[setup, side]
        far = table[:, 4:5]
        near[side] = jnp.broadcast_to(DAMP * far / (1.0 + 6.0 * far), (nb, 128))
        for face in range(4):
            hot = jnp.where(table[:, face:face + 1] == lane_nb.astype(F32), 1.0, 0.0)
            ohn[side, face * nb:(face + 1) * nb] = jnp.concatenate([hot, hot], axis=1).astype(BF16)

    for off in range(1, n_sp):
        spread_landed(off)

    @pl.when(k > 0)
    def _():
        spread_landed(0)

    for off in range(1, n_sp):
        slots_landed(off)
    slots = jnp.sum(jnp.where(spot, slots_in[:, :1], 0.0), axis=2, keepdims=True)
    slots = jnp.broadcast_to(slots, (n_sp, bk, nb)).reshape(rows, nb)
    take = jnp.where(slots == iota((rows, nb), 1).astype(F32), 1.0, 0.0).T.astype(BF16)

    def settled(value):
        high, low = split(value)
        return dot(take, high) + dot(take, low)

    bs[...] = settled(br[...].reshape(rows, CELLS))

    def hand_copy(it):
        return pltpu.make_async_remote_copy(
            src_ref=hsrc.at[it], dst_ref=hand.at[it], send_sem=ts_sem.at[it], recv_sem=tr_sem.at[it],
            device_id=(lax.rem(k + 1, n_tm), s), device_id_type=MESH)

    def back_copy():
        return pltpu.make_async_remote_copy(
            src_ref=hsrc.at[ITERS - 1], dst_ref=st.at[0], send_sem=ts_sem.at[ITERS - 1],
            recv_sem=tr_sem.at[ITERS - 1], device_id=(lax.rem(k + n_tm - 1, n_tm), s),
            device_id_type=MESH)

    @pl.when(k > 0)
    def _():
        hsrc[ITERS - 1] = bs[...]
        back_copy().start()

    def coarse_copy(it, off):
        return pltpu.make_async_remote_copy(
            src_ref=cs.at[it], dst_ref=cr.at[it, k], send_sem=cs_sem.at[it, off],
            recv_sem=cr_sem.at[it, k], device_id=(lax.rem(k + off, n_tm), s), device_id_type=MESH)

    def coarse_landed(it, origin):
        pltpu.make_async_remote_copy(
            src_ref=cs.at[it], dst_ref=cr.at[it, origin], send_sem=cs_sem.at[it, 0],
            recv_sem=cr_sem.at[it, origin], device_id=(lax.rem(k + 1, n_tm), s),
            device_id_type=MESH).wait_recv()

    def iteration(it, carry):
        drive(bs[...] + source_ref[0, 0])

        def one(v, c):
            vcycle((it * 2 + v) * 2)

            @pl.when(v == 0)
            def _():
                f_ref[0] = xs[...]
                drive(xs[...] + source_ref[0, 1])
            return c

        lax.fori_loop(0, 2, one, 0)

        @pl.when((it == 0) & (k < n_tm - 1))
        def _():
            back_copy().wait_recv()

        @pl.when((it == 0) & (k == n_tm - 1))
        def _():
            for off in range(1, n_sp):
                own_landed(off)
            st[0] = settled(gr[...].reshape(rows, CELLS))

        residual = xs[...] - st[it]
        cs[it] = restrict(residual)
        for off in range(1, n_tm):
            @pl.when(k + off < n_tm)
            def _():
                coarse_copy(it, off).start()

        @pl.when((k < n_tm - 1) & (it < ITERS - 1))
        def _():
            hsrc[it] = xs[...]
            hand_copy(it).start()

        zs[...] = jnp.zeros_like(zs)
        ps[...] = jnp.zeros_like(ps)
        for j in range(n_tm - 1):
            @pl.when(j < k)
            def _():
                coarse_landed(it, j)
                pushed = classes(zs[...], ms)
                ps[...] = pushed
                zs[...] = pushed + cr[it, j]
        st[it + 1] = st[it] + (prolong(classes(zs[...], ms)) + residual)

        @pl.when((k > 0) & (it < ITERS - 1))
        def _():
            hand_copy(it).wait_recv()
            bs[...] = hand[it] + prolong(ps[...])
        return carry

    lax.fori_loop(0, ITERS, iteration, 0)
    c_ref[0] = st[ITERS]

    for off in range(1, n_sp):
        slots_copy(off).wait_send()

    @pl.when(k == n_tm - 1)
    def _():
        for off in range(1, n_sp):
            own_copy(off).wait_send()

    @pl.when(k > 0)
    def _():
        back_copy().wait_send()

    @pl.when(k == 0)
    def _():
        for off in range(1, n_sp):
            spread_copy(ib, is_sem, off, k).wait_send()

    @pl.when(k < n_tm - 1)
    def _():
        for off in range(n_sp):
            spread_copy(gb, ps_sem, off, lax.rem(k + 1, n_tm)).wait_send()

    def drain(slot, carry):
        @pl.when(s < n_sp - 1)
        def _():
            halo_up(slot).wait_send()

        @pl.when(s > 0)
        def _():
            halo_down(slot).wait_send()
        return carry

    lax.fori_loop(0, setup + 1, drain, 0)
    for it in range(ITERS):
        if it < ITERS - 1:
            @pl.when(k < n_tm - 1)
            def _():
                hand_copy(it).wait_send()
        for off in range(1, n_tm):
            @pl.when(k + off < n_tm)
            def _():
                coarse_copy(it, off).wait_send()


def solution(mesh):
    n_tm, n_sp = mesh.shape["tm"], mesh.shape["space"]

    def body(init_state, guess, source, remap, neighbors, block_class, step_number, inverse, cstep):
        nb = init_state.shape[0]
        bk = -(-(2 * nb // n_sp) // 8) * 8
        slots = ITERS * 4 + 1
        dma = pltpu.SemaphoreType.DMA
        out = jax.ShapeDtypeStruct((1, nb, CELLS), F32)
        return pl.pallas_call(
            functools.partial(kernel, n_tm, n_sp, bk),
            name="mgrit",
            out_shape=(out, out),
            in_specs=[pl.BlockSpec(memory_space=pltpu.VMEM)] * 9,
            out_specs=[pl.BlockSpec(memory_space=pltpu.VMEM)] * 2,
            scratch_shapes=[
                pltpu.VMEM((n_sp, bk, CELLS), F32),
                pltpu.VMEM((n_sp, bk, CELLS), F32),
                pltpu.VMEM((n_sp, bk, CELLS), F32),
                pltpu.VMEM((n_sp, bk, CELLS), F32),
                pltpu.VMEM((slots, 2, nb, 128), F32),
                pltpu.VMEM((slots, 2, nb, 128), F32),
                pltpu.VMEM((ITERS + 1, nb, CELLS), F32),
                pltpu.VMEM((ITERS, nb, CELLS), F32),
                pltpu.VMEM((ITERS, nb, CELLS), F32),
                pltpu.VMEM((ITERS, nb, 128), F32),
                pltpu.VMEM((ITERS, n_tm, nb, 128), F32),
                pltpu.VMEM((4 * nb, 2 * nb), BF16),
                pltpu.VMEM((2, 4 * nb, 2 * nb), BF16),
                pltpu.VMEM((nb, 2 * nb), BF16),
                pltpu.VMEM((nb, 2 * nb), BF16),
                pltpu.VMEM((nb, 2 * nb), BF16),
                pltpu.VMEM((nb, 2 * nb), BF16),
                pltpu.VMEM((CELLS, 128), BF16),
                pltpu.VMEM((128, CELLS), BF16),
                pltpu.VMEM((4 * COARSE, CLASSES * COARSE), BF16),
                pltpu.VMEM((4 * COARSE, CLASSES * COARSE), BF16),
                pltpu.VMEM((nb, CELLS), F32),
                pltpu.VMEM((nb, CELLS), F32),
                pltpu.VMEM((nb, CELLS), F32),
                pltpu.VMEM((nb, 128), F32),
                pltpu.VMEM((nb, 128), F32),
                pltpu.VMEM((3, nb, 128), F32),
                pltpu.VMEM((2, nb, 128), F32),
                pltpu.VMEM((n_sp, 8, 128), F32),
                pltpu.VMEM((n_sp, 8, 128), F32),
                dma((n_sp,)), dma((n_sp,)),
                dma((n_sp,)), dma((n_sp,)), dma((n_sp,)), dma((n_sp,)), dma((n_sp,)),
                dma((slots, 2)), dma((slots, 2)),
                dma((ITERS,)), dma((ITERS,)),
                dma((ITERS, n_tm)), dma((ITERS, n_tm)),
            ],
            compiler_params=pltpu.CompilerParams(collective_id=0, has_side_effects=True),
        )(
            init_state, guess, source, remap.reshape(1, nb), neighbors, block_class.reshape(1, nb),
            step_number.reshape(1, CLASSES), inverse.reshape(CLASSES * COARSE, COARSE),
            cstep.reshape(CLASSES * COARSE, COARSE),
        )

    placed = (
        P("space", None), P("tm", "space", None), P("tm", None, "space", None), P("space"),
        P("space", None), P("space"), P(), P(), P(),
    )
    return jax.shard_map(
        body, mesh=mesh, in_specs=placed,
        out_specs=(P("tm", "space", None), P("tm", "space", None)), check_vma=False,
    )
```

```python
import functools

import jax
import jax.numpy as jnp
from jax import lax
from jax.experimental import pallas as pl
from jax.experimental.pallas import tpu as pltpu
from jax.sharding import PartitionSpec as P

CELLS = 512
COARSE = 64
CLASSES = 4
ITERS = 2
DAMP = 0.8
MESH = pl.DeviceIdType.MESH
F32 = jnp.float32
BF16 = jnp.bfloat16


def split(value):
    high = value.astype(BF16)
    return high, (value - high.astype(F32)).astype(BF16)


def dot(left, right):
    return jnp.dot(left, right, preferred_element_type=F32)


def roll(value, shift):
    shift = shift % 128
    return value if shift == 0 else pltpu.roll(value, shift, 1)


def iota(shape, dim):
    return lax.broadcasted_iota(jnp.int32, shape, dim)


def kernel(
    n_tm, n_sp, bk,
    init_ref, guess_ref, source_ref, remap_ref, nb_ref, class_ref, step_ref, inv_ref, cstep_ref,
    c_ref, f_ref,
    gb, ib, gr, br, hs, hr, st, hsrc, hand, cs, cr,
    ohl, ohn, oh4, oh5, oh4t, oh5t, rm, pm, mi, ms, xs, ws, bs, zs, ps, scale, near,
    slots_out, slots_in, so_sem, si_sem,
    gs_sem, gr_sem, ps_sem, is_sem, br_sem, hs_sem, hr_sem, ts_sem, tr_sem, cs_sem, cr_sem,
):
    k = lax.axis_index("tm")
    s = lax.axis_index("space")
    nb = init_ref.shape[0]
    rows = n_sp * bk
    bits = nb.bit_length() - 1
    setup = ITERS * 4

    hr[...] = jnp.zeros_like(hr)
    barrier = pltpu.get_barrier_semaphore()
    for off in range(1, n_sp):
        pl.semaphore_signal(barrier, inc=1, device_id=(k, lax.rem(s + off, n_sp)), device_id_type=MESH)
    for off in range(1, n_tm):
        pl.semaphore_signal(barrier, inc=1, device_id=(lax.rem(k + off, n_tm), s), device_id_type=MESH)

    @pl.when(k < n_tm - 1)
    def _():
        for off in range(1, n_sp):
            pl.semaphore_signal(barrier, inc=1, device_id=(k + 1, lax.rem(s + off, n_sp)), device_id_type=MESH)

    @pl.when(k > 0)
    def _():
        for off in range(1, n_sp):
            pl.semaphore_signal(barrier, inc=1, device_id=(k - 1, lax.rem(s + off, n_sp)), device_id_type=MESH)

    eye = iota((nb, nb), 0) == iota((nb, nb), 1)

    def column(row):
        return jnp.sum(jnp.where(eye, row, 0.0), axis=1, keepdims=True)

    remap_row = remap_ref[...]
    target_row = lax.shift_right_logical(remap_row, bits)
    slot_row = (remap_row - lax.shift_left(target_row, bits)).astype(F32)
    target_f = target_row.astype(F32)
    same = (column(target_f) == target_f) & (iota((nb, nb), 0) < iota((nb, nb), 1))
    pos_row = jnp.sum(jnp.where(same, 1.0, 0.0), axis=0, keepdims=True)
    send_row = target_f * float(bk) + pos_row
    chosen = iota((rows, nb), 0).astype(F32) == send_row
    send_mat = jnp.where(chosen, 1.0, 0.0)
    slot_col = jnp.sum(jnp.where(chosen, slot_row + 1.0, 0.0), axis=1, keepdims=True) - 1.0
    send_mat = jnp.concatenate([send_mat, send_mat], axis=1).astype(BF16)

    def bucketed(value):
        return dot(send_mat, jnp.concatenate(split(value), axis=0)).reshape(n_sp, bk, CELLS)

    spot = iota((n_sp, bk, 128), 1) == iota((n_sp, bk, 128), 2)
    slot_wide = jnp.broadcast_to(slot_col, (rows, 128)).reshape(n_sp, bk, 128)
    slot_lanes = jnp.sum(jnp.where(spot, slot_wide, 0.0), axis=1, keepdims=True)
    slots_out[...] = jnp.broadcast_to(slot_lanes, (n_sp, 8, 128))
    gb[...] = bucketed(guess_ref[0])

    @pl.when(k == 0)
    def _():
        ib[...] = bucketed(init_ref[...])

    sides = jnp.minimum(k, 1) + jnp.minimum(n_tm - 1 - k, 1)
    pl.semaphore_wait(barrier, (n_sp - 1) * (1 + sides) + n_tm - 1)

    def spread_copy(src, ssem, off, col):
        to = lax.rem(s + off, n_sp)
        return pltpu.make_async_remote_copy(
            src_ref=src.at[to], dst_ref=br.at[s], send_sem=ssem.at[off], recv_sem=br_sem.at[s],
            device_id=(col, to), device_id_type=MESH)

    def own_copy(off):
        to = lax.rem(s + off, n_sp)
        return pltpu.make_async_remote_copy(
            src_ref=gb.at[to], dst_ref=gr.at[s], send_sem=gs_sem.at[off],
            recv_sem=gr_sem.at[s], device_id=(k, to), device_id_type=MESH)

    def spread_landed(off):
        origin = lax.rem(s + off, n_sp)
        pltpu.make_async_remote_copy(
            src_ref=gb.at[origin], dst_ref=br.at[origin], send_sem=ps_sem.at[off],
            recv_sem=br_sem.at[origin], device_id=(lax.rem(k + 1, n_tm), origin),
            device_id_type=MESH).wait_recv()

    def own_landed(off):
        origin = lax.rem(s + off, n_sp)
        pltpu.make_async_remote_copy(
            src_ref=gb.at[origin], dst_ref=gr.at[origin],
            send_sem=gs_sem.at[off], recv_sem=gr_sem.at[origin], device_id=(k, origin),
            device_id_type=MESH).wait_recv()

    def slots_copy(off):
        to = lax.rem(s + off, n_sp)
        return pltpu.make_async_remote_copy(
            src_ref=slots_out.at[to], dst_ref=slots_in.at[s], send_sem=so_sem.at[off],
            recv_sem=si_sem.at[s], device_id=(k, to), device_id_type=MESH)

    def slots_landed(off):
        origin = lax.rem(s + off, n_sp)
        pltpu.make_async_remote_copy(
            src_ref=slots_out.at[origin], dst_ref=slots_in.at[origin], send_sem=so_sem.at[off],
            recv_sem=si_sem.at[origin], device_id=(k, origin), device_id_type=MESH).wait_recv()

    for off in range(1, n_sp):
        slots_copy(off).start()
    slots_in[s] = slots_out[s]

    @pl.when(k == 0)
    def _():
        for off in range(1, n_sp):
            spread_copy(ib, is_sem, off, k).start()
        br[s] = ib[s]

    @pl.when(k < n_tm - 1)
    def _():
        for off in range(n_sp):
            spread_copy(gb, ps_sem, off, lax.rem(k + 1, n_tm)).start()

    class_col = column(class_ref[...].astype(F32))
    diffusion = jnp.zeros((nb, 1), F32)
    for cl in range(CLASSES):
        diffusion = diffusion + jnp.where(class_col == float(cl), step_ref[:, cl:cl + 1], 0.0)
    dif = jnp.broadcast_to(diffusion, (nb, 128))
    scale[0] = DAMP * dif / (1.0 + 6.0 * dif)
    scale[1] = DAMP / (1.0 + 6.0 * dif)
    scale[2] = (1.0 + 6.0 * dif) / DAMP
    lane = iota((nb, 128), 1)
    linked = [column(nb_ref[face:face + 1, :].astype(F32)).astype(jnp.int32) for face in range(6)]
    table = jnp.where(lane == 4, dif, -1.0)
    for face in range(4):
        table = jnp.where(lane == face, (linked[face] - s * nb).astype(F32), table)
    hs[setup, 0] = table
    hs[setup, 1] = table

    def halo_up(slot):
        return pltpu.make_async_remote_copy(
            src_ref=hs.at[slot, 0], dst_ref=hr.at[slot, 0], send_sem=hs_sem.at[slot, 0],
            recv_sem=hr_sem.at[slot, 0], device_id=(k, lax.rem(s + 1, n_sp)), device_id_type=MESH)

    def halo_down(slot):
        return pltpu.make_async_remote_copy(
            src_ref=hs.at[slot, 1], dst_ref=hr.at[slot, 1], send_sem=hs_sem.at[slot, 1],
            recv_sem=hr_sem.at[slot, 1], device_id=(k, lax.rem(s + n_sp - 1, n_sp)), device_id_type=MESH)

    def exchange(slot):
        @pl.when(s < n_sp - 1)
        def _():
            halo_up(slot).start()

        @pl.when(s > 0)
        def _():
            halo_down(slot).start()

    def exchanged(slot):
        @pl.when(s > 0)
        def _():
            halo_up(slot).wait_recv()

        @pl.when(s < n_sp - 1)
        def _():
            halo_down(slot).wait_recv()

    exchange(setup)
    gr[s] = gb[s]

    lane_nb = iota((nb, nb), 1)
    for face in range(6):
        shift = s * nb + (0 if face < 4 else (-nb if face == 4 else nb))
        ids = linked[face]
        hot = jnp.where((ids - shift == lane_nb) & (ids >= 0), 1.0, 0.0)
        if face >= 4:
            turned = hot.T
            turned = jnp.concatenate([turned, turned], axis=1).astype(BF16)
            (oh4t if face == 4 else oh5t)[...] = turned
        hot = jnp.concatenate([hot, hot], axis=1).astype(BF16)
        if face < 4:
            ohl[face * nb:(face + 1) * nb] = hot
        elif face == 4:
            oh4[...] = hot
        else:
            oh5[...] = hot

    def parent(cell):
        return (lax.shift_right_logical(cell, 7) * 16
                + (lax.shift_right_logical(cell, 4) & 3) * 4
                + lax.shift_right_logical(cell & 7, 1))

    rm[...] = jnp.where(parent(iota((CELLS, 128), 0)) == iota((CELLS, 128), 1), 0.125, 0.0).astype(BF16)
    pm[...] = jnp.where(parent(iota((128, CELLS), 1)) == (iota((128, CELLS), 0) & 63), 1.0, 0.0).astype(BF16)
    for src, dst in ((inv_ref, mi), (cstep_ref, ms)):
        high, low = split(src[...].T)
        dst[...] = jnp.concatenate([high, high, low, jnp.zeros_like(low)], axis=0)

    zz = lane & 7
    yy = lax.shift_right_logical(lane, 3) & 7
    left = lane < 64

    def classes(coarse, mat):
        high = coarse.astype(BF16).astype(F32)
        both = high + roll(coarse - high, 64)
        product = dot(jnp.concatenate([both, high], axis=1).astype(BF16), mat[...])
        low_c = jnp.where(left, 0.0, 1.0)
        picked = (jnp.where(class_col == low_c, product[:, :128], 0.0)
                  + jnp.where(class_col == low_c + 2.0, product[:, 128:], 0.0))
        return jnp.where(left, picked + roll(picked, 64), 0.0)

    def prolong(coarse):
        high = coarse.astype(BF16).astype(F32)
        return dot((high + roll(coarse - high, 64)).astype(BF16), pm[...])

    def restrict(value):
        both = dot(jnp.concatenate(split(value), axis=0), rm[...])
        return both[:nb] + both[nb:]

    def tiles_of(value):
        return [value[:, 128 * j:128 * j + 128] for j in range(4)]

    def gathered(hot, value):
        return dot(hot, jnp.concatenate(split(value), axis=0))

    def planes(tiles):
        top = bottom = jnp.zeros((nb, 128), F32)
        for j in range(4):
            top = jnp.where(zz == j, roll(tiles[j], j - 7), top)
            top = jnp.where(zz == 4 + j, roll(tiles[j], j - 2), top)
            bottom = jnp.where(zz == j, roll(tiles[j], j), bottom)
            bottom = jnp.where(zz == 4 + j, roll(tiles[j], j + 3), bottom)
        return top, bottom

    def plane_step(plane, driven, side, cross):
        w = gathered(ohn[side], plane)
        turned = roll(plane, 64)
        total = turned + jnp.where(
            left, jnp.where(zz == 0, roll(w[:nb], -67), roll(turned, 1)),
            jnp.where(zz == 3, roll(w[nb:2 * nb], 67), roll(turned, -1)))
        total = total + jnp.where(yy == 0, roll(w[2 * nb:3 * nb], -56), roll(plane, 8))
        total = total + jnp.where(yy == 7, roll(w[3 * nb:], 56), roll(plane, -8))
        total = total + roll(plane, -4) + cross
        return (1.0 - DAMP) * plane + driven + near[side] * total

    def inside(tiles):
        xface = jnp.where(left, roll(tiles[3], 64), roll(tiles[0], 64))
        yface = jnp.zeros((nb, 128), F32)
        for j in range(4):
            yface = jnp.where(yy == j, roll(tiles[j], 8 * j - 56), yface)
            yface = jnp.where(yy == 4 + j, roll(tiles[j], 32 + 8 * j), yface)
        ghosts = gathered(ohl[...], jnp.concatenate([xface, yface], axis=1))
        turned = [roll(tile, 64) for tile in tiles]
        turned = [ghosts[:nb, :128]] + turned + [ghosts[nb:2 * nb, :128]]
        g2 = ghosts[2 * nb:3 * nb, 128:]
        g3 = ghosts[3 * nb:, 128:]
        sums = []
        for j in range(4):
            total = turned[j + 1] + jnp.where(left, turned[j], turned[j + 2])
            total = total + jnp.where(yy == 0, roll(g2, -8 * j), roll(tiles[j], 8))
            total = total + jnp.where(yy == 7, roll(g3, 24 - 8 * j), roll(tiles[j], -8))
            total = total + jnp.where(zz == 0, 0.0, roll(tiles[j], 1))
            total = total + jnp.where(zz == 7, 0.0, roll(tiles[j], -1))
            sums.append(total)
        return sums

    def with_ends(sums, below, above):
        g4 = gathered(oh4[...], below)
        g5 = gathered(oh5[...], above)
        return [
            sums[j] + jnp.where(zz == 0, roll(g4, -j), 0.0) + jnp.where(zz == 7, roll(g5, 7 - j), 0.0)
            for j in range(4)
        ]

    def swept(tiles, driven, sums):
        return [(1.0 - DAMP) * tiles[j] + driven[j] + scale[0] * sums[j] for j in range(4)]

    def vcycle(base):
        driven = tiles_of(ws[...])
        for stage in range(2):
            slot = base + stage
            tiles = driven if stage == 0 else tiles_of(xs[...])
            top, bottom = planes(tiles)
            hs[slot, 0] = top
            hs[slot, 1] = bottom
            exchange(slot)
            for off in range(1, n_sp):
                turn = (off - 1) * 4 // (n_sp - 1)

                @pl.when((k == n_tm - 1) & (slot == turn))
                def _():
                    own_copy(off).start()
            sums = inside(tiles)
            up_cross = gathered(oh4t[...], bottom)
            down_cross = gathered(oh5t[...], top)
            exchanged(slot)
            below, above = hr[slot, 0], hr[slot, 1]
            tiles = swept(tiles, driven, with_ends(sums, below, above))
            below = plane_step(below, hr[base, 0], 0, up_cross)
            above = plane_step(above, hr[base, 1], 1, down_cross)
            sums = with_ends(inside(tiles), below, above)
            if stage == 0:
                rest = jnp.concatenate(
                    [driven[j] - DAMP * tiles[j] + scale[0] * sums[j] for j in range(4)], axis=1)
                fix = prolong(classes(scale[2] * restrict(rest), mi))
                xs[...] = jnp.concatenate(tiles, axis=1) + fix
            else:
                xs[...] = jnp.concatenate(swept(tiles, driven, sums), axis=1)

    def drive(value):
        ws[...] = value * jnp.concatenate([scale[1]] * 4, axis=1)

    exchanged(setup)
    for side in range(2):
        table = hr[setup, side]
        far = table[:, 4:5]
        near[side] = jnp.broadcast_to(DAMP * far / (1.0 + 6.0 * far), (nb, 128))
        for face in range(4):
            hot = jnp.where(table[:, face:face + 1] == lane_nb.astype(F32), 1.0, 0.0)
            ohn[side, face * nb:(face + 1) * nb] = jnp.concatenate([hot, hot], axis=1).astype(BF16)

    for off in range(1, n_sp):
        spread_landed(off)

    @pl.when(k > 0)
    def _():
        spread_landed(0)

    for off in range(1, n_sp):
        slots_landed(off)
    slots = jnp.sum(jnp.where(spot, slots_in[:, :1], 0.0), axis=2, keepdims=True)
    slots = jnp.broadcast_to(slots, (n_sp, bk, nb)).reshape(rows, nb)
    take = jnp.where(slots == iota((rows, nb), 1).astype(F32), 1.0, 0.0).T.astype(BF16)

    def settled(value):
        high, low = split(value)
        return dot(take, high) + dot(take, low)

    bs[...] = settled(br[...].reshape(rows, CELLS))

    def hand_copy(it):
        return pltpu.make_async_remote_copy(
            src_ref=hsrc.at[it], dst_ref=hand.at[it], send_sem=ts_sem.at[it], recv_sem=tr_sem.at[it],
            device_id=(lax.rem(k + 1, n_tm), s), device_id_type=MESH)

    def back_copy():
        return pltpu.make_async_remote_copy(
            src_ref=hsrc.at[ITERS - 1], dst_ref=st.at[0], send_sem=ts_sem.at[ITERS - 1],
            recv_sem=tr_sem.at[ITERS - 1], device_id=(lax.rem(k + n_tm - 1, n_tm), s),
            device_id_type=MESH)

    @pl.when(k > 0)
    def _():
        hsrc[ITERS - 1] = bs[...]
        back_copy().start()

    def coarse_copy(it, off):
        return pltpu.make_async_remote_copy(
            src_ref=cs.at[it], dst_ref=cr.at[it, k], send_sem=cs_sem.at[it, off],
            recv_sem=cr_sem.at[it, k], device_id=(lax.rem(k + off, n_tm), s), device_id_type=MESH)

    def coarse_landed(it, origin):
        pltpu.make_async_remote_copy(
            src_ref=cs.at[it], dst_ref=cr.at[it, origin], send_sem=cs_sem.at[it, 0],
            recv_sem=cr_sem.at[it, origin], device_id=(lax.rem(k + 1, n_tm), s),
            device_id_type=MESH).wait_recv()

    def iteration(it, carry):
        drive(bs[...] + source_ref[0, 0])

        def one(v, c):
            vcycle((it * 2 + v) * 2)

            @pl.when(v == 0)
            def _():
                f_ref[0] = xs[...]
                drive(xs[...] + source_ref[0, 1])
            return c

        lax.fori_loop(0, 2, one, 0)

        @pl.when((it == 0) & (k < n_tm - 1))
        def _():
            back_copy().wait_recv()

        @pl.when((it == 0) & (k == n_tm - 1))
        def _():
            for off in range(1, n_sp):
                own_landed(off)
            st[0] = settled(gr[...].reshape(rows, CELLS))

        residual = xs[...] - st[it]
        cs[it] = restrict(residual)
        for off in range(1, n_tm):
            @pl.when(k + off < n_tm)
            def _():
                coarse_copy(it, off).start()

        @pl.when((k < n_tm - 1) & (it < ITERS - 1))
        def _():
            hsrc[it] = xs[...]
            hand_copy(it).start()

        zs[...] = jnp.zeros_like(zs)
        ps[...] = jnp.zeros_like(ps)
        for j in range(n_tm - 1):
            @pl.when(j < k)
            def _():
                coarse_landed(it, j)
                pushed = classes(zs[...], ms)
                ps[...] = pushed
                zs[...] = pushed + cr[it, j]
        st[it + 1] = st[it] + (prolong(classes(zs[...], ms)) + residual)

        @pl.when((k > 0) & (it < ITERS - 1))
        def _():
            hand_copy(it).wait_recv()
            bs[...] = hand[it] + prolong(ps[...])
        return carry

    lax.fori_loop(0, ITERS, iteration, 0)
    c_ref[0] = st[ITERS]

    for off in range(1, n_sp):
        slots_copy(off).wait_send()

    @pl.when(k == n_tm - 1)
    def _():
        for off in range(1, n_sp):
            own_copy(off).wait_send()

    @pl.when(k > 0)
    def _():
        back_copy().wait_send()

    @pl.when(k == 0)
    def _():
        for off in range(1, n_sp):
            spread_copy(ib, is_sem, off, k).wait_send()

    @pl.when(k < n_tm - 1)
    def _():
        for off in range(n_sp):
            spread_copy(gb, ps_sem, off, lax.rem(k + 1, n_tm)).wait_send()

    def drain(slot, carry):
        @pl.when(s < n_sp - 1)
        def _():
            halo_up(slot).wait_send()

        @pl.when(s > 0)
        def _():
            halo_down(slot).wait_send()
        return carry

    lax.fori_loop(0, setup + 1, drain, 0)
    for it in range(ITERS):
        if it < ITERS - 1:
            @pl.when(k < n_tm - 1)
            def _():
                hand_copy(it).wait_send()
        for off in range(1, n_tm):
            @pl.when(k + off < n_tm)
            def _():
                coarse_copy(it, off).wait_send()


def solution(mesh):
    n_tm, n_sp = mesh.shape["tm"], mesh.shape["space"]

    def body(init_state, guess, source, remap, neighbors, block_class, step_number, inverse, cstep):
        nb = init_state.shape[0]
        bk = -(-(2 * nb // n_sp) // 8) * 8
        slots = ITERS * 4 + 1
        dma = pltpu.SemaphoreType.DMA
        out = jax.ShapeDtypeStruct((1, nb, CELLS), F32)
        return pl.pallas_call(
            functools.partial(kernel, n_tm, n_sp, bk),
            name="mgrit",
            out_shape=(out, out),
            in_specs=[pl.BlockSpec(memory_space=pltpu.VMEM)] * 9,
            out_specs=[pl.BlockSpec(memory_space=pltpu.VMEM)] * 2,
            scratch_shapes=[
                pltpu.VMEM((n_sp, bk, CELLS), F32),
                pltpu.VMEM((n_sp, bk, CELLS), F32),
                pltpu.VMEM((n_sp, bk, CELLS), F32),
                pltpu.VMEM((n_sp, bk, CELLS), F32),
                pltpu.VMEM((slots, 2, nb, 128), F32),
                pltpu.VMEM((slots, 2, nb, 128), F32),
                pltpu.VMEM((ITERS + 1, nb, CELLS), F32),
                pltpu.VMEM((ITERS, nb, CELLS), F32),
                pltpu.VMEM((ITERS, nb, CELLS), F32),
                pltpu.VMEM((ITERS, nb, 128), F32),
                pltpu.VMEM((ITERS, n_tm, nb, 128), F32),
                pltpu.VMEM((4 * nb, 2 * nb), BF16),
                pltpu.VMEM((2, 4 * nb, 2 * nb), BF16),
                pltpu.VMEM((nb, 2 * nb), BF16),
                pltpu.VMEM((nb, 2 * nb), BF16),
                pltpu.VMEM((nb, 2 * nb), BF16),
                pltpu.VMEM((nb, 2 * nb), BF16),
                pltpu.VMEM((CELLS, 128), BF16),
                pltpu.VMEM((128, CELLS), BF16),
                pltpu.VMEM((4 * COARSE, CLASSES * COARSE), BF16),
                pltpu.VMEM((4 * COARSE, CLASSES * COARSE), BF16),
                pltpu.VMEM((nb, CELLS), F32),
                pltpu.VMEM((nb, CELLS), F32),
                pltpu.VMEM((nb, CELLS), F32),
                pltpu.VMEM((nb, 128), F32),
                pltpu.VMEM((nb, 128), F32),
                pltpu.VMEM((3, nb, 128), F32),
                pltpu.VMEM((2, nb, 128), F32),
                pltpu.VMEM((n_sp, 8, 128), F32),
                pltpu.VMEM((n_sp, 8, 128), F32),
                dma((n_sp,)), dma((n_sp,)),
                dma((n_sp,)), dma((n_sp,)), dma((n_sp,)), dma((n_sp,)), dma((n_sp,)),
                dma((slots, 2)), dma((slots, 2)),
                dma((ITERS,)), dma((ITERS,)),
                dma((ITERS, n_tm)), dma((ITERS, n_tm)),
            ],
            compiler_params=pltpu.CompilerParams(collective_id=0, has_side_effects=True),
        )(
            init_state, guess, source, remap.reshape(1, nb), neighbors.T, block_class.reshape(1, nb),
            step_number.reshape(1, CLASSES), inverse.reshape(CLASSES * COARSE, COARSE),
            cstep.reshape(CLASSES * COARSE, COARSE),
        )

    placed = (
        P("space", None), P("tm", "space", None), P("tm", None, "space", None), P("space"),
        P("space", None), P("space"), P(), P(), P(),
    )
    return jax.shard_map(
        body, mesh=mesh, in_specs=placed,
        out_specs=(P("tm", "space", None), P("tm", "space", None)), check_vma=False,
    )
```
